128 devices in a mesh: dp: 32 (over y, z, core), section: 4 (over x).
Axes of the slice: x: 4, y: 4, z: 4, core: 2. Of those that a mesh axis runs over, the one named last changes fastest.
Arguments:
- hidden_in: bfloat16 [2, 2048, 8192], P(None, 'dp'), may hold values from -6 to 6
- out_grad: bfloat16 [2, 2048, 8192], P(None, 'dp'), may hold values from -0.4375 to 0.4375
- gains: float32 [2, 4, 4096], P(None, 'section'), may hold values from 0.1 to 1.9
- blocks: bfloat16 [2, 4, 256, 128, 128], P(None, 'section'), may hold values from -0.1875 to 0.1875
- block_rows: int32 [2, 4, 256], P(None, 'section'), may hold values from 0 to 31, as said below
- block_cols: int32 [2, 4, 256], P(None, 'section'), may hold values from 0 to 31, as said below
- block_counts: int32 [2, 4], P(None, 'section'), may hold values from 64 to 256, as said below
Outputs:
- block_grads: bfloat16 [2, 4, 256, 128, 128], P(None, 'section', 'dp')
The draws below stay inside these ranges and needn't reach their ends.
Inputs may be any that keep to these rules, and one draw needn't show every extreme that they name: Slot n of layer (t, s) is the tile at block row block_rows[t, s, n]; the 256 slots of one layer name different tiles. `block_cols`: block column of each slot, paired with block_rows. `block_counts`: only slots below a layer's count hold weights; the others are padding. Counts differ between layers; in every draw one layer has 256 live slots and another a quarter of 256.
All inputs are finite; a program needn't handle non-finite values.
Results may differ from the reference program's by a relative error of at most 0.023.
Values may be sent and summed in bfloat16 or wider, within the bound.
No kernel may reach another device: no remote copies, remote signals or barrier semaphores. Data moves between devices by JAX's collectives and lax.ppermute only.
A program may use at most 320 MiB of HBM per device.

```python
import jax
import jax.numpy as jnp
from jax import lax

D = 8192
WIN = 4096
BLK = 128
GRID = 32
NNZ_MAX = 256
LAYERS_DEV = 2
MB = 2
TOK_DEV = 64
TOKENS = 2048
LAYERS = 8
N_DP = 32
N_SECTION = 4


def slot_ids(key):
    base_key = jax.random.fold_in(key, 17)
    key_list = jax.random.split(base_key, LAYERS_DEV * N_SECTION)
    shuffled = jax.vmap(lambda one_key: jax.random.permutation(one_key, GRID * GRID)[:NNZ_MAX])(key_list)
    return shuffled.reshape(LAYERS_DEV, N_SECTION, NNZ_MAX).astype(jnp.int32)


def draw_block_rows(key, part):
    return (slot_ids(key) // GRID).astype(jnp.int32)


def draw_block_cols(key, part):
    return (slot_ids(key) % GRID).astype(jnp.int32)


def draw_block_counts(key, part):
    slot_total = LAYERS_DEV * N_SECTION
    key_list = jax.random.split(jax.random.fold_in(key, 29), 3)
    counts = jax.random.randint(key_list[0], (slot_total,), NNZ_MAX // 4, NNZ_MAX + 1)
    heavy_slot = jax.random.randint(key_list[1], (), 0, slot_total)
    light_slot = (heavy_slot + 1 + jax.random.randint(key_list[2], (), 0, slot_total - 1)) % slot_total
    positions = jnp.arange(slot_total)
    counts = jnp.where(positions == heavy_slot, NNZ_MAX, counts)
    counts = jnp.where(positions == light_slot, NNZ_MAX // 4, counts)
    return counts.reshape(LAYERS_DEV, N_SECTION).astype(jnp.int32)


def with_spikes(drawn, rng, source, target, parts, factor):
    def block_of(dim):
        return (jnp.arange(drawn.shape[dim]) // (drawn.shape[dim] // parts)).reshape((-1,) + (1,) * (drawn.ndim - 1 - dim))

    near = jax.random.permutation(rng, parts)[block_of(target)]
    second = (block_of(target) + parts // 2) % parts
    return jnp.where((block_of(source) == near) | (block_of(source) == second), factor * drawn, drawn)


def level_of(rng, extent, cuts, smallest, top_value):
    gain, own = 1.0, jax.random.fold_in(rng, 6)
    for dim, shards_of in cuts:
        heights = jnp.exp(jax.random.uniform(jax.random.fold_in(own, dim), (shards_of,), jnp.float32, smallest / len(cuts), top_value / len(cuts)))
        gain = gain * jnp.repeat(heights, extent[dim] // shards_of).reshape([-1 if axis == dim else 1 for axis in range(len(extent))])
    return gain


def centred(rng, dims, scale, limit, shards=(), held_as=jnp.bfloat16):
    drawn = scale * jax.random.normal(rng, dims, jnp.float32)
    if shards:
        drawn = drawn * level_of(rng, dims, shards, -0.22, 0.18)
    return jnp.clip(drawn, -limit, limit).astype(held_as)


def heavy_noise(own_key, shape, spread, reach, cuts, heavy, kind=jnp.bfloat16):
    drawn = spread * jax.random.normal(own_key, shape, jnp.float32)
    if cuts:
        drawn = drawn * level_of(own_key, shape, cuts, -0.22, 0.18)
    return jnp.clip(with_spikes(drawn, jax.random.fold_in(own_key, 3), *heavy), -reach, reach).astype(kind)


def setup_inputs(seed: int = 0) -> dict:
    seeds = jax.random.split(jax.random.key(seed), 8)
    hidden_in = centred(seeds[0], (MB, TOKENS, D), 1.0, 6.0, ((1, 32),))
    out_grad = heavy_noise(seeds[1], (MB, TOKENS, D), (1.0 / (MB * TOKENS) ** 0.5), 0.4375, ((1, 32),), (1, 2, 32, 2.75))
    gains = jnp.clip(1.0 + 0.18 * jax.random.normal(seeds[2], (LAYERS_DEV, N_SECTION, WIN), jnp.float32), 0.1, 1.9)
    blocks = centred(seeds[3], (LAYERS_DEV, N_SECTION, NNZ_MAX, BLK, BLK), (NNZ_MAX * BLK // GRID) ** -0.5, 0.1875, ((1, 4),))
    block_rows = draw_block_rows(jax.random.fold_in(seeds[7], 71), 0)
    block_cols = draw_block_cols(jax.random.fold_in(seeds[7], 71), 0)
    block_counts = draw_block_counts(jax.random.fold_in(seeds[7], 71), 0)
    return dict(hidden_in=hidden_in, out_grad=out_grad, gains=gains, blocks=blocks, block_rows=block_rows, block_cols=block_cols, block_counts=block_counts)


norm_eps = 1e-05

def inverse_rms(values):
    return lax.rsqrt(lax.optimization_barrier(jnp.mean(values * values, axis=-1, keepdims=True)) + norm_eps)

def sparse_apply(normed, tiles, rows_list, cols_list, live_mask):
    token_rows = normed.shape[0]
    pieces = normed.reshape(token_rows, GRID, BLK)[:, rows_list, :].astype(jnp.float32)
    products = jnp.einsum('tnk,nkj->tnj', pieces, tiles.astype(jnp.float32), precision=lax.Precision.HIGHEST)
    products = products * live_mask[None, :, None]
    placed = jnp.zeros((token_rows, GRID, BLK), jnp.float32).at[:, cols_list, :].add(products)
    return placed.reshape(token_rows, WIN)

def sparse_transpose(tile_error, tiles, rows_list, cols_list, live_mask):
    token_rows = tile_error.shape[0]
    pieces = tile_error.reshape(token_rows, GRID, BLK)[:, cols_list, :].astype(jnp.float32)
    products = jnp.einsum('tnj,nkj->tnk', pieces, tiles.astype(jnp.float32), precision=lax.Precision.HIGHEST)
    products = products * live_mask[None, :, None]
    placed = jnp.zeros((token_rows, GRID, BLK), jnp.float32).at[:, rows_list, :].add(products)
    return placed.reshape(token_rows, WIN)

def forward_layer(layer_in, gain_row, tiles, rows_list, cols_list, live_mask, start_in, start_out):
    as_float = layer_in.astype(jnp.float32)
    inv_rms = inverse_rms(as_float)
    normed = (as_float[:, start_in:start_in + WIN] * inv_rms * gain_row).astype(jnp.bfloat16)
    mixed_out = sparse_apply(normed, tiles, rows_list, cols_list, live_mask)
    updated = (as_float[:, start_out:start_out + WIN] + jax.nn.silu(mixed_out)).astype(jnp.bfloat16)
    return (layer_in.at[:, start_out:start_out + WIN].set(updated), normed, mixed_out)

def backward_layer(grad_in, layer_in, mixed_out, gain_row, tiles, rows_list, cols_list, live_mask, start_in, start_out):
    as_float = layer_in.astype(jnp.float32)
    inv_rms = inverse_rms(as_float)
    upstream = grad_in.astype(jnp.float32)
    sigmoid_u = jax.nn.sigmoid(mixed_out)
    tile_error = (upstream[:, start_out:start_out + WIN] * sigmoid_u * (1.0 + mixed_out * (1.0 - sigmoid_u))).astype(jnp.bfloat16)
    grad_normed = sparse_transpose(tile_error, tiles, rows_list, cols_list, live_mask)
    weighted = grad_normed * gain_row
    inner_sum = lax.optimization_barrier(jnp.sum(weighted * as_float[:, start_in:start_in + WIN], axis=-1, keepdims=True))
    result = upstream - inv_rms * inv_rms * inv_rms / D * inner_sum * as_float
    result = result.at[:, start_in:start_in + WIN].add(inv_rms * weighted)
    return (result.astype(jnp.bfloat16), tile_error)

def reference(hidden_in, out_grad, gains, blocks, block_rows, block_cols, block_counts):
    layer_info = []
    for layer_pos in range(LAYERS):
        turn_pos = layer_pos // N_SECTION
        section_pos = layer_pos % N_SECTION
        parity = layer_pos % 2
        live_mask = (jnp.arange(NNZ_MAX, dtype=jnp.int32) < block_counts[turn_pos, section_pos]).astype(jnp.float32)
        layer_info.append((gains[turn_pos, section_pos], blocks[turn_pos, section_pos], block_rows[turn_pos, section_pos], block_cols[turn_pos, section_pos], live_mask, parity * WIN, (1 - parity) * WIN))
    normed_store = [[] for layer_pos in range(LAYERS)]
    error_store = [[] for layer_pos in range(LAYERS)]
    for which_batch in range(MB):
        hidden = hidden_in[which_batch]
        saved = []
        for layer_pos in range(LAYERS):
            gain_row, tiles, rows_list, cols_list, live_mask, start_in, start_out = layer_info[layer_pos]
            following, normed, mixed_out = forward_layer(hidden, gain_row, tiles, rows_list, cols_list, live_mask, start_in, start_out)
            saved.append((hidden, normed, mixed_out))
            hidden = following
        gradient = out_grad[which_batch]
        for layer_pos in reversed(range(LAYERS)):
            gain_row, tiles, rows_list, cols_list, live_mask, start_in, start_out = layer_info[layer_pos]
            layer_in, normed, mixed_out = saved[layer_pos]
            gradient, tile_error = backward_layer(gradient, layer_in, mixed_out, gain_row, tiles, rows_list, cols_list, live_mask, start_in, start_out)
            normed_store[layer_pos].append(normed)
            error_store[layer_pos].append(tile_error)
    results = []
    for layer_pos in range(LAYERS):
        gain_row, tiles, rows_list, cols_list, live_mask, start_in, start_out = layer_info[layer_pos]
        normed_all = jnp.stack(normed_store[layer_pos]).reshape(MB, N_DP, TOK_DEV, WIN)
        normed_all = normed_all.transpose(1, 0, 2, 3).reshape(N_DP, MB * TOK_DEV, WIN)
        error_all = jnp.stack(error_store[layer_pos]).reshape(MB, N_DP, TOK_DEV, WIN)
        error_all = error_all.transpose(1, 0, 2, 3).reshape(N_DP, MB * TOK_DEV, WIN)

        def add_device(running, pair):
            normed_dev, error_dev = pair
            normed_tiles = normed_dev.reshape(-1, GRID, BLK)[:, rows_list, :].astype(jnp.float32)
            error_tiles = error_dev.reshape(-1, GRID, BLK)[:, cols_list, :].astype(jnp.float32)
            partial_sum = jnp.einsum('tnk,tnj->nkj', normed_tiles, error_tiles, precision=lax.Precision.HIGHEST)
            partial_sum = partial_sum * live_mask[:, None, None]
            rounded = lax.optimization_barrier(partial_sum.astype(jnp.bfloat16))
            return (running + rounded.astype(jnp.float32), None)
        summed, unused_out = lax.scan(add_device, jnp.zeros((NNZ_MAX, BLK, BLK), jnp.float32), (normed_all, error_all))
        results.append(summed.astype(jnp.bfloat16))
    return jnp.stack(results).reshape(LAYERS_DEV, N_SECTION, NNZ_MAX, BLK, BLK)
```

```python
import jax
import jax.numpy as jnp
from jax import lax
from jax.experimental import pallas as pl
from jax.experimental.pallas import tpu as pltpu
from jax.sharding import PartitionSpec as P

norm_eps = 1e-05
LAG = 1
UNROLL = 32
f32 = jnp.float32
bf16 = jnp.bfloat16
VM = pl.BlockSpec(memory_space=pltpu.VMEM)
SM = pl.BlockSpec(memory_space=pltpu.SMEM)
ANY = pl.BlockSpec(memory_space=pl.ANY)
LIMIT = 48 * 2**20


def split_pair(value, width):
    high = value.astype(bf16).astype(f32)
    low = value - high
    lane = lax.broadcasted_iota(jnp.int32, (value.shape[0], width), 1)
    return jnp.where(lane == 0, high, jnp.where(lane == 1, low, 0.0)).astype(bf16)


def tile_loop(table, turn, slots, groups, gather_at, scatter_at, source, weights, acc, transposed):
    dims = (((1,), (1 if transposed else 0,)), ((), ()))

    def group(g, carry):
        for k in range(UNROLL):
            n = turn * slots + g * UNROLL + k
            got = table[gather_at + n]
            put = table[scatter_at + n]
            acc[put] += lax.dot_general(source[got], weights[n], dims, preferred_element_type=f32)
        return carry

    lax.fori_loop(0, groups, group, 0)


class Plan:
    def __init__(self, sections, turns, slots, tile, grid, tokens):
        self.sections, self.turns, self.slots = sections, turns, slots
        self.tile, self.grid = tile, grid
        self.units = sections * LAG
        self.rows = tokens // self.units
        self.span = (sections - 1) * LAG
        self.ticks = turns * self.units + self.span
        self.row_get, self.col_get = 0, turns * slots
        self.row_put, self.col_put = 2 * turns * slots, 3 * turns * slots
        self.groups = 4 * turns * slots
        self.counts = self.groups + turns
        self.section = self.counts + turns
        self.half = self.section + 1

    def piece(self, dtype, extra=0):
        return jax.ShapeDtypeStruct((self.grid + extra, self.rows, self.tile), dtype)


def forward_tick(plan, tick, table, entering, square0, gains, weights, prev, critical, early, stores):
    G, T, B, M = plan.grid, plan.rows, plan.tile, plan.units
    width = 2 * G * B
    use_entering = tick < M + plan.span
    use_prev = tick >= M
    named = dict(table=table, entering=entering if use_entering else None, square0=square0 if tick < M else None,
                 gains=gains, weights=weights, prev=prev if use_prev else None, critical=critical, early=early)
    names = [name for name in named if named[name] is not None]
    turns_here = [turn for turn in range(2) if (use_entering if turn == 0 else use_prev)]
    count_in = len(names)

    def kernel(*refs):
        ref = dict(zip(names, refs))
        store_out = dict(zip(turns_here, refs[count_in + len(turns_here) + 4:]))
        sent, kept, slope, scale = refs[count_in + len(turns_here):][:4]
        normed, acc, sem = refs[-3:]
        tab = ref["table"]
        step = tick - LAG * tab[plan.section]
        active = (step >= 0) & (step < 2 * M)

        @pl.when(active)
        def _():
            turn = jnp.where(step >= M, 1, 0)
            unit = step - turn * M
            squares = jnp.zeros((T, B), f32)
            for b in range(G):
                cut = slice(b * B, (b + 1) * B)
                if use_entering:
                    value = ref["entering"][unit, :, cut].astype(f32)
                if use_prev:
                    older = ref["prev"][b].astype(f32)
                    value = jnp.where(turn == 0, value, older) if use_entering else older
                if early is not None:
                    value = value + ref["early"][b].astype(f32)
                if critical is not None:
                    value = value + ref["critical"][b].astype(f32)
                value = value.astype(bf16)
                kept[b] = value
                value = value.astype(f32)
                squares = squares + value * value
            own = jnp.sum(squares, axis=-1, keepdims=True)
            total = own
            if critical is not None:
                total = total + jnp.sum(ref["critical"][G].astype(f32), axis=-1, keepdims=True)
            if tick < M:
                total = total + jnp.sum(ref["square0"][unit], axis=-1, keepdims=True)
            inv_rms = lax.rsqrt(total / width + norm_eps)
            scale[...] = jnp.broadcast_to(inv_rms, (T, B))
            for b in range(G):
                gain = ref["gains"][turn * G + b]
                normed[b] = (kept[b].astype(f32) * inv_rms * gain).astype(bf16)
            for place in turns_here:
                @pl.when(turn == place)
                def _():
                    pltpu.make_async_copy(normed, store_out[place].at[unit], sem).start()
            acc[...] = jnp.zeros_like(acc)
            tile_loop(tab, turn, plan.slots, tab[plan.groups + turn], plan.row_get, plan.col_put, normed, ref["weights"], acc, False)
            pltpu.make_async_copy(normed, store_out[turns_here[0]].at[unit], sem).wait()
            for b in range(G):
                mixed = acc[b]
                gate = jax.nn.sigmoid(mixed)
                sent[b] = (mixed * gate).astype(bf16)
                slope[b] = (gate * (1.0 + mixed * (1.0 - gate))).astype(bf16)
            sent[G] = split_pair(own, B)

        @pl.when(jnp.logical_not(active))
        def _():
            sent[...] = jnp.zeros_like(sent)

    ins = [named[name] for name in names] + [stores[turn] for turn in turns_here]
    outs = pl.pallas_call(
        kernel,
        in_specs=[SM] + [VM] * (count_in - 1) + [ANY] * len(turns_here),
        out_specs=[VM] * 4 + [ANY] * len(turns_here),
        out_shape=[plan.piece(bf16, 1), plan.piece(bf16), plan.piece(bf16), jax.ShapeDtypeStruct((T, B), f32)]
        + [jax.ShapeDtypeStruct(stores[turn].shape, bf16) for turn in turns_here],
        input_output_aliases={count_in + i: 4 + i for i in range(len(turns_here))},
        scratch_shapes=[pltpu.VMEM((G, T, B), bf16), pltpu.VMEM((G + 1, T, B), f32), pltpu.SemaphoreType.DMA],
        compiler_params=pltpu.CompilerParams(vmem_limit_bytes=LIMIT),
        name="forward_tick",
    )(*ins)
    stores = list(stores)
    for i, turn in enumerate(turns_here):
        stores[turn] = outs[4 + i]
    return outs[0], (outs[1], outs[2], outs[3]), stores


def backward_tick(plan, tick, table, entering, gains, weights, saved, prev, critical, early, stores):
    G, T, B, M = plan.grid, plan.rows, plan.tile, plan.units
    width = 2 * G * B
    back = plan.ticks - 1 - tick
    use_entering = back < M + plan.span
    use_prev = back >= M
    named = dict(table=table, entering=entering if use_entering else None, gains=gains, weights=weights,
                 kept=saved[0], slope=saved[1], scale=saved[2],
                 prev=prev if use_prev else None, critical=critical, early=early)
    names = [name for name in named if named[name] is not None]
    turns_here = [turn for turn in range(2) if (use_entering if turn == 1 else use_prev)]
    count_in = len(names)

    def kernel(*refs):
        ref = dict(zip(names, refs))
        sent, grad = refs[count_in + len(turns_here):][:2]
        store_out = dict(zip(turns_here, refs[count_in + len(turns_here) + 2:]))
        error, acc, sem = refs[-3:]
        tab = ref["table"]
        step = tick - LAG * tab[plan.section]
        active = (step >= 0) & (step < 2 * M)

        @pl.when(active)
        def _():
            turn = jnp.where(step >= M, 1, 0)
            unit = step - turn * M
            for b in range(G):
                cut = slice(b * B, (b + 1) * B)
                if use_entering:
                    value = ref["entering"][unit, :, cut].astype(f32)
                if use_prev:
                    older = ref["prev"][b].astype(f32)
                    value = jnp.where(turn == 1, value, older) if use_entering else older
                if early is not None:
                    value = value + ref["early"][b].astype(f32)
                if critical is not None:
                    value = value + ref["critical"][b].astype(f32)
                value = value.astype(bf16)
                grad[b] = value
                error[b] = (value.astype(f32) * ref["slope"][b].astype(f32)).astype(bf16)
            for place in turns_here:
                @pl.when(turn == place)
                def _():
                    pltpu.make_async_copy(error, store_out[place].at[unit], sem).start()
            acc[...] = jnp.zeros_like(acc)
            tile_loop(tab, turn, plan.slots, tab[plan.groups + turn], plan.col_get, plan.row_put, error, ref["weights"], acc, True)
            pltpu.make_async_copy(error, store_out[turns_here[0]].at[unit], sem).wait()
            inner = jnp.zeros((T, B), f32)
            for b in range(G):
                weighted = acc[b] * ref["gains"][turn * G + b]
                acc[b] = weighted
                inner = inner + weighted * ref["kept"][b].astype(f32)
            inv_rms = ref["scale"][:, 0:1]
            own = inv_rms * inv_rms * inv_rms / width * jnp.sum(inner, axis=-1, keepdims=True)
            total = own
            if critical is not None:
                total = total + jnp.sum(ref["critical"][G].astype(f32), axis=-1, keepdims=True)
            for b in range(G):
                sent[b] = (inv_rms * acc[b] - total * ref["kept"][b].astype(f32)).astype(bf16)
            sent[G] = split_pair(own, B)

        @pl.when(jnp.logical_not(active))
        def _():
            sent[...] = jnp.zeros_like(sent)

    ins = [named[name] for name in names] + [stores[turn] for turn in turns_here]
    outs = pl.pallas_call(
        kernel,
        in_specs=[SM] + [VM] * (count_in - 1) + [ANY] * len(turns_here),
        out_specs=[VM] * 2 + [ANY] * len(turns_here),
        out_shape=[plan.piece(bf16, 1), plan.piece(bf16)]
        + [jax.ShapeDtypeStruct(stores[turn].shape, bf16) for turn in turns_here],
        input_output_aliases={count_in + i: 2 + i for i in range(len(turns_here))},
        scratch_shapes=[pltpu.VMEM((G, T, B), bf16), pltpu.VMEM((G + 1, T, B), f32), pltpu.SemaphoreType.DMA],
        compiler_params=pltpu.CompilerParams(vmem_limit_bytes=LIMIT),
        name="backward_tick",
    )(*ins)
    stores = list(stores)
    for i, turn in enumerate(turns_here):
        stores[turn] = outs[2 + i]
    return outs[0], outs[1], stores


def tile_grads(plan, turn, table, normed_pair, error_pair, share, parts):
    G, T, B, M = plan.grid, plan.rows, plan.tile, plan.units
    local = plan.slots // parts
    steps = 8
    chunk = local // steps
    tokens = M * T

    def kernel(tab, *refs):
        normeds, errors = refs[:parts], refs[parts:2 * parts]
        out, turned, flat = refs[2 * parts:]
        step = pl.program_id(0)

        @pl.when(step == 0)
        def _():
            for b in range(G):
                for p in range(parts):
                    for m in range(M):
                        at = p * tokens + m * T
                        flat[b, at:at + T, :] = errors[p][m, b]
                    whole = jnp.concatenate([normeds[p][m, b] for m in range(M)], axis=0)
                    turned[b, :, p * tokens:(p + 1) * tokens] = whole.T

        half = tab[plan.half]
        live = tab[plan.counts + turn]
        for k in range(chunk):
            i = step * chunk + k
            n = (i // share) * (share * parts) + half * share + i % share
            at = turn * plan.slots + n
            made = jnp.dot(turned[tab[plan.row_get + at]], flat[tab[plan.col_get + at]], preferred_element_type=f32)
            out[k] = jnp.where(n < live, made, 0.0).astype(bf16)

    whole = pl.BlockSpec((M, G, T, B), lambda i, tab: (0, 0, 0, 0))
    return pl.pallas_call(
        kernel,
        grid_spec=pltpu.PrefetchScalarGridSpec(
            num_scalar_prefetch=1,
            grid=(steps,),
            in_specs=[whole] * (2 * parts),
            out_specs=pl.BlockSpec((chunk, B, B), lambda i, tab: (i, 0, 0)),
            scratch_shapes=[pltpu.VMEM((G, B, parts * tokens), bf16), pltpu.VMEM((G, parts * tokens, B), bf16)],
        ),
        out_shape=jax.ShapeDtypeStruct((local, B, B), bf16),
        compiler_params=pltpu.CompilerParams(vmem_limit_bytes=LIMIT),
        name="tile_grads",
    )(table, *normed_pair, *error_pair)


def body(hidden_in, out_grad, gains, blocks, block_rows, block_cols, block_counts):
    sections = lax.axis_size("section")
    replicas = lax.axis_size("dp")
    section_pos = lax.axis_index("section").astype(jnp.int32)
    core = (lax.axis_index("dp") % 2).astype(jnp.int32)
    turns, slots, tile = blocks.shape[0], blocks.shape[2], blocks.shape[3]
    tokens = hidden_in.shape[0] * hidden_in.shape[1]
    half_width = hidden_in.shape[2] // 2
    grid = half_width // tile
    plan = Plan(sections, turns, slots, tile, grid, tokens)
    M, T = plan.units, plan.rows

    rows_list, cols_list, counts = block_rows[:, 0], block_cols[:, 0], block_counts[:, 0]
    live = jnp.arange(slots, dtype=jnp.int32)[None] < counts[:, None]
    table = jnp.concatenate([
        rows_list.reshape(-1), cols_list.reshape(-1),
        jnp.where(live, rows_list, grid).reshape(-1), jnp.where(live, cols_list, grid).reshape(-1),
        (counts + UNROLL - 1) // UNROLL, counts, section_pos[None], core[None],
    ])
    parity = section_pos % 2
    hidden = hidden_in.reshape(M, T, 2 * half_width)
    entering = lax.dynamic_slice_in_dim(hidden, parity * half_width, half_width, 2)
    entering_grad = lax.dynamic_slice_in_dim(
        out_grad.reshape(M, T, 2 * half_width), (1 - parity) * half_width, half_width, 2
    )
    other = hidden[:, :, half_width:].astype(f32)
    square0 = jnp.where(section_pos == 0, jnp.sum(other * other, axis=-1, keepdims=True), 0.0)
    square0 = jnp.pad(square0, ((0, 0), (0, 0), (0, tile - 1)))
    weights = blocks.reshape(turns * slots, tile, tile)
    gain_rows = gains.reshape(turns * grid, 1, tile)

    def ring(part, by):
        return lax.ppermute(part, "section", [(i, (i + by) % sections) for i in range(sections)])

    empty = jnp.zeros((M, grid, T, tile), bf16)
    stores = [empty, empty]
    ahead, behind, saved = {}, {}, {}
    for tick in range(plan.ticks):
        prev = saved[tick - M][0] if tick >= M else None
        sent, saved[tick], stores = forward_tick(
            plan, tick, table, entering, square0, gain_rows, weights, prev,
            ahead.get(tick - LAG), behind.get(tick - plan.span), stores,
        )
        if tick + LAG < plan.ticks:
            ahead[tick] = ring(sent, 1)
        if tick + plan.span < plan.ticks:
            behind[tick] = ring(sent, -1)
    normed = stores

    swap = [(i, i ^ 1) for i in range(replicas)]
    share = slots // replicas

    def finish(turn, error):
        pairs = []
        for own in (normed[turn], error):
            other_core = lax.ppermute(own, "dp", swap)
            pairs.append([own, other_core])
        part = tile_grads(plan, turn, table, pairs[0], pairs[1], share, 2)
        groups = [[i for i in range(replicas) if i % 2 == c] for c in range(2)]
        return lax.psum_scatter(part, "dp", scatter_dimension=0, axis_index_groups=groups, tiled=True)

    stores = [empty, empty]
    ahead, behind, grads = {}, {}, {}
    results = [None] * turns
    for back in range(plan.ticks):
        tick = plan.ticks - 1 - back
        sent, grads[back], stores = backward_tick(
            plan, tick, table, entering_grad, gain_rows, weights, saved[tick], grads.get(back - M),
            ahead.get(back - LAG), behind.get(back - plan.span), stores,
        )
        if back + LAG < plan.ticks:
            ahead[back] = ring(sent, -1)
        if back + plan.span < plan.ticks:
            behind[back] = ring(sent, 1)
        if back == M + plan.span - 1:
            results[1] = finish(1, stores[1])
    results[0] = finish(0, stores[0])
    return jnp.stack(results)[:, None]


def solution(mesh):
    return jax.shard_map(
        body,
        mesh=mesh,
        in_specs=(
            P(None, "dp", None),
            P(None, "dp", None),
            P(None, "section", None),
            P(None, "section", None, None, None),
            P(None, "section", None),
            P(None, "section", None),
            P(None, "section"),
        ),
        out_specs=P(None, "section", "dp", None, None),
        check_vma=False,
    )
```

```python
import jax
import jax.numpy as jnp
from jax import lax
from jax.experimental import pallas as pl
from jax.experimental.pallas import tpu as pltpu
from jax.sharding import PartitionSpec as P

norm_eps = 1e-05
LAG = 1
UNROLL = 32
f32 = jnp.float32
bf16 = jnp.bfloat16
VM = pl.BlockSpec(memory_space=pltpu.VMEM)
SM = pl.BlockSpec(memory_space=pltpu.SMEM)
HBM = pl.BlockSpec(memory_space=pltpu.HBM)
LIMIT = 6 * 2**20
GRAD_LIMIT = 12 * 2**20


def split_pair(value, width):
    high = value.astype(bf16).astype(f32)
    low = value - high
    lane = lax.broadcasted_iota(jnp.int32, (value.shape[0], width), 1)
    return jnp.where(lane == 0, high, jnp.where(lane == 1, low, 0.0)).astype(bf16)


def tile_loop(table, turn, slots, groups, gather_at, scatter_at, source, weights, acc, transposed):
    dims = (((1,), (1 if transposed else 0,)), ((), ()))

    def group(g, carry):
        for k in range(UNROLL):
            n = turn * slots + g * UNROLL + k
            got = table[gather_at + n]
            put = table[scatter_at + n]
            acc[put] += lax.dot_general(source[got], weights[n], dims, preferred_element_type=f32)
        return carry

    lax.fori_loop(0, groups, group, 0)


class Plan:
    def __init__(self, sections, turns, slots, tile, grid, tokens):
        self.sections, self.turns, self.slots = sections, turns, slots
        self.tile, self.grid = tile, grid
        self.units = sections * LAG
        self.rows = tokens // self.units
        self.span = (sections - 1) * LAG
        self.ticks = turns * self.units + self.span
        self.row_get, self.col_get = 0, turns * slots
        self.row_put, self.col_put = 2 * turns * slots, 3 * turns * slots
        self.groups = 4 * turns * slots
        self.counts = self.groups + turns
        self.section = self.counts + turns
        self.half = self.section + 1

    def piece(self, dtype, extra=0):
        return jax.ShapeDtypeStruct((self.grid + extra, self.rows, self.tile), dtype)


def forward_tick(plan, tick, table, entering, square0, gains, weights, prev, critical, early, stores):
    G, T, B, M = plan.grid, plan.rows, plan.tile, plan.units
    width = 2 * G * B
    use_entering = tick < M + plan.span
    use_prev = tick >= M
    named = dict(table=table, entering=entering if use_entering else None, square0=square0 if tick < M else None,
                 gains=gains, weights=weights, prev=prev if use_prev else None, critical=critical, early=early)
    names = [name for name in named if named[name] is not None]
    given = len(names) + sum(stores[turn] is not None for turn in range(2) if (use_entering if turn == 0 else use_prev))
    turns_here = [turn for turn in range(2) if (use_entering if turn == 0 else use_prev)]
    count_in = len(names)

    def kernel(*refs):
        ref = dict(zip(names, refs))
        store_out = dict(zip(turns_here, refs[given + 4:]))
        sent, kept_out, slope_out, scale_out = refs[given:][:4]
        normed, acc, kept, slope, scale, sems = refs[-6:]
        tab = ref["table"]
        step = tick - LAG * tab[plan.section]
        active = (step >= 0) & (step < 2 * M)

        @pl.when(active)
        def _():
            turn = jnp.where(step >= M, 1, 0)
            unit = step - turn * M
            squares = jnp.zeros((T, B), f32)
            for b in range(G):
                cut = slice(b * B, (b + 1) * B)
                if use_entering:
                    value = ref["entering"][unit, :, cut].astype(f32)
                if use_prev:
                    older = ref["prev"][b].astype(f32)
                    value = jnp.where(turn == 0, value, older) if use_entering else older
                if early is not None:
                    value = value + ref["early"][b].astype(f32)
                if critical is not None:
                    value = value + ref["critical"][b].astype(f32)
                value = value.astype(bf16)
                kept[b] = value
                value = value.astype(f32)
                squares = squares + value * value
            own = jnp.sum(squares, axis=-1, keepdims=True)
            total = own
            if critical is not None:
                total = total + jnp.sum(ref["critical"][G].astype(f32), axis=-1, keepdims=True)
            if tick < M:
                total = total + jnp.sum(ref["square0"][unit], axis=-1, keepdims=True)
            inv_rms = lax.rsqrt(total / width + norm_eps)
            scale[...] = jnp.broadcast_to(inv_rms, (T, B))
            for b in range(G):
                gain = ref["gains"][turn * G + b]
                normed[b] = (kept[b].astype(f32) * inv_rms * gain).astype(bf16)
            for place in turns_here:
                @pl.when(turn == place)
                def _():
                    pltpu.make_async_copy(normed, store_out[place].at[unit], sems.at[0]).start()
            keep = [pltpu.make_async_copy(kept, kept_out, sems.at[1]), pltpu.make_async_copy(scale, scale_out, sems.at[2])]
            for copy in keep:
                copy.start()
            acc[...] = jnp.zeros_like(acc)
            tile_loop(tab, turn, plan.slots, tab[plan.groups + turn], plan.row_get, plan.col_put, normed, ref["weights"], acc, False)
            for b in range(G):
                mixed = acc[b]
                gate = jax.nn.sigmoid(mixed)
                sent[b] = (mixed * gate).astype(bf16)
                slope[b] = (gate * (1.0 + mixed * (1.0 - gate))).astype(bf16)
                if b % (G // 2) == G // 2 - 1:
                    part = pl.ds(b + 1 - G // 2, G // 2)
                    keep.append(pltpu.make_async_copy(slope.at[part], slope_out.at[part], sems.at[3 + b // (G // 2)]))
                    keep[-1].start()
            sent[G] = split_pair(own, B)
            pltpu.make_async_copy(normed, store_out[turns_here[0]].at[unit], sems.at[0]).wait()
            for copy in keep:
                copy.wait()

        @pl.when(jnp.logical_not(active))
        def _():
            sent[...] = jnp.zeros_like(sent)

    held = [turn for turn in turns_here if stores[turn] is not None]
    ins = [named[name] for name in names] + [stores[turn] for turn in held]
    outs = pl.pallas_call(
        kernel,
        in_specs=[SM] + [VM] * (count_in - 1) + [HBM] * len(held),
        out_specs=[VM] + [HBM] * (3 + len(turns_here)),
        out_shape=[plan.piece(bf16, 1), pltpu.HBM((G, T, B), bf16), pltpu.HBM((G, T, B), bf16), pltpu.HBM((T, B), f32)]
        + [pltpu.HBM((M, G, T, B), bf16)] * len(turns_here),
        input_output_aliases={count_in + i: 4 + turns_here.index(turn) for i, turn in enumerate(held)},
        scratch_shapes=[pltpu.VMEM((G, T, B), bf16), pltpu.VMEM((G + 1, T, B), f32), pltpu.VMEM((G, T, B), bf16),
                        pltpu.VMEM((G, T, B), bf16), pltpu.VMEM((T, B), f32), pltpu.SemaphoreType.DMA((5,))],
        compiler_params=pltpu.CompilerParams(vmem_limit_bytes=LIMIT),
        name="forward_tick",
    )(*ins)
    stores = list(stores)
    for i, turn in enumerate(turns_here):
        stores[turn] = outs[4 + i]
    return outs[0], (outs[1], outs[2], outs[3]), stores


def backward_tick(plan, tick, table, entering, gains, weights, saved, prev, critical, early, stores):
    G, T, B, M = plan.grid, plan.rows, plan.tile, plan.units
    width = 2 * G * B
    back = plan.ticks - 1 - tick
    use_entering = back < M + plan.span
    use_prev = back >= M
    named = dict(table=table, entering=entering if use_entering else None, gains=gains, weights=weights,
                 kept=saved[0], slope=saved[1], scale=saved[2],
                 prev=prev if use_prev else None, critical=critical, early=early)
    names = [name for name in named if named[name] is not None]
    given = len(names) + sum(stores[turn] is not None for turn in range(2) if (use_entering if turn == 1 else use_prev))
    turns_here = [turn for turn in range(2) if (use_entering if turn == 1 else use_prev)]
    count_in = len(names)

    def kernel(*refs):
        ref = dict(zip(names, refs))
        sent, grad_out = refs[given:][:2]
        store_out = dict(zip(turns_here, refs[given + 2:]))
        error, acc, grad, sems = refs[-4:]
        tab = ref["table"]
        step = tick - LAG * tab[plan.section]
        active = (step >= 0) & (step < 2 * M)

        @pl.when(active)
        def _():
            turn = jnp.where(step >= M, 1, 0)
            unit = step - turn * M
            for b in range(G):
                cut = slice(b * B, (b + 1) * B)
                if use_entering:
                    value = ref["entering"][unit, :, cut].astype(f32)
                if use_prev:
                    older = ref["prev"][b].astype(f32)
                    value = jnp.where(turn == 1, value, older) if use_entering else older
                if early is not None:
                    value = value + ref["early"][b].astype(f32)
                if critical is not None:
                    value = value + ref["critical"][b].astype(f32)
                value = value.astype(bf16)
                grad[b] = value
                error[b] = (value.astype(f32) * ref["slope"][b].astype(f32)).astype(bf16)
            for place in turns_here:
                @pl.when(turn == place)
                def _():
                    pltpu.make_async_copy(error, store_out[place].at[unit], sems.at[0]).start()
            keep = pltpu.make_async_copy(grad, grad_out, sems.at[1])
            keep.start()
            acc[...] = jnp.zeros_like(acc)
            tile_loop(tab, turn, plan.slots, tab[plan.groups + turn], plan.col_get, plan.row_put, error, ref["weights"], acc, True)
            inner = jnp.zeros((T, B), f32)
            for b in range(G):
                weighted = acc[b] * ref["gains"][turn * G + b]
                acc[b] = weighted
                inner = inner + weighted * ref["kept"][b].astype(f32)
            inv_rms = ref["scale"][:, 0:1]
            own = inv_rms * inv_rms * inv_rms / width * jnp.sum(inner, axis=-1, keepdims=True)
            total = own
            if critical is not None:
                total = total + jnp.sum(ref["critical"][G].astype(f32), axis=-1, keepdims=True)
            for b in range(G):
                sent[b] = (inv_rms * acc[b] - total * ref["kept"][b].astype(f32)).astype(bf16)
            sent[G] = split_pair(own, B)
            pltpu.make_async_copy(error, store_out[turns_here[0]].at[unit], sems.at[0]).wait()
            keep.wait()

        @pl.when(jnp.logical_not(active))
        def _():
            sent[...] = jnp.zeros_like(sent)

    held = [turn for turn in turns_here if stores[turn] is not None]
    ins = [named[name] for name in names] + [stores[turn] for turn in held]
    outs = pl.pallas_call(
        kernel,
        in_specs=[SM] + [VM] * (count_in - 1) + [HBM] * len(held),
        out_specs=[VM] + [HBM] * (1 + len(turns_here)),
        out_shape=[plan.piece(bf16, 1), pltpu.HBM((G, T, B), bf16)]
        + [pltpu.HBM((M, G, T, B), bf16)] * len(turns_here),
        input_output_aliases={count_in + i: 2 + turns_here.index(turn) for i, turn in enumerate(held)},
        scratch_shapes=[pltpu.VMEM((G, T, B), bf16), pltpu.VMEM((G + 1, T, B), f32), pltpu.VMEM((G, T, B), bf16),
                        pltpu.SemaphoreType.DMA((2,))],
        compiler_params=pltpu.CompilerParams(vmem_limit_bytes=LIMIT),
        name="backward_tick",
    )(*ins)
    stores = list(stores)
    for i, turn in enumerate(turns_here):
        stores[turn] = outs[2 + i]
    return outs[0], outs[1], stores


def tile_grads(plan, turn, table, normed_pair, error_pair, share, parts):
    G, T, B, M = plan.grid, plan.rows, plan.tile, plan.units
    local = plan.slots // parts
    steps = 8
    chunk = local // steps
    tokens = M * T

    def kernel(tab, *refs):
        normeds, errors = refs[:parts], refs[parts:2 * parts]
        out, turned, flat = refs[2 * parts:]
        step = pl.program_id(0)

        @pl.when(step == 0)
        def _():
            for b in range(G):
                for p in range(parts):
                    for m in range(M):
                        at = p * tokens + m * T
                        flat[b, at:at + T, :] = errors[p][m, b]
                    whole = jnp.concatenate([normeds[p][m, b] for m in range(M)], axis=0)
                    turned[b, :, p * tokens:(p + 1) * tokens] = whole.T

        half = tab[plan.half]
        live = tab[plan.counts + turn]
        for k in range(chunk):
            i = step * chunk + k
            n = (i // share) * (share * parts) + half * share + i % share
            at = turn * plan.slots + n
            made = jnp.dot(turned[tab[plan.row_get + at]], flat[tab[plan.col_get + at]], preferred_element_type=f32)
            out[k] = jnp.where(n < live, made, 0.0).astype(bf16)

    whole = pl.BlockSpec((M, G, T, B), lambda i, tab: (0, 0, 0, 0))
    return pl.pallas_call(
        kernel,
        grid_spec=pltpu.PrefetchScalarGridSpec(
            num_scalar_prefetch=1,
            grid=(steps,),
            in_specs=[whole] * (2 * parts),
            out_specs=pl.BlockSpec((chunk, B, B), lambda i, tab: (i, 0, 0)),
            scratch_shapes=[pltpu.VMEM((G, B, parts * tokens), bf16), pltpu.VMEM((G, parts * tokens, B), bf16)],
        ),
        out_shape=jax.ShapeDtypeStruct((local, B, B), bf16),
        compiler_params=pltpu.CompilerParams(vmem_limit_bytes=GRAD_LIMIT),
        name="tile_grads",
    )(table, *normed_pair, *error_pair)


def sum_parts(parts):
    def kernel(given, out):
        total = given[0].astype(f32)
        for i in range(1, parts.shape[0]):
            total = total + given[i].astype(f32)
        out[...] = total.astype(bf16)

    rest = parts.shape[2:]
    return pl.pallas_call(
        kernel,
        grid=(parts.shape[1] // 2,),
        in_specs=[pl.BlockSpec((parts.shape[0], 2, *rest), lambda i: (0, i, 0, 0))],
        out_specs=pl.BlockSpec((2, *rest), lambda i: (i, 0, 0)),
        out_shape=jax.ShapeDtypeStruct(parts.shape[1:], bf16),
        compiler_params=pltpu.CompilerParams(vmem_limit_bytes=GRAD_LIMIT),
        name="sum_parts",
    )(parts)


def body(hidden_in, out_grad, gains, blocks, block_rows, block_cols, block_counts):
    sections = lax.axis_size("section")
    replicas = lax.axis_size("dp")
    section_pos = lax.axis_index("section").astype(jnp.int32)
    core = (lax.axis_index("dp") % 2).astype(jnp.int32)
    turns, slots, tile = blocks.shape[0], blocks.shape[2], blocks.shape[3]
    tokens = hidden_in.shape[0] * hidden_in.shape[1]
    half_width = hidden_in.shape[2] // 2
    grid = half_width // tile
    plan = Plan(sections, turns, slots, tile, grid, tokens)
    M, T = plan.units, plan.rows

    rows_list, cols_list, counts = block_rows[:, 0], block_cols[:, 0], block_counts[:, 0]
    live = jnp.arange(slots, dtype=jnp.int32)[None] < counts[:, None]
    table = jnp.concatenate([
        rows_list.reshape(-1), cols_list.reshape(-1),
        jnp.where(live, rows_list, grid).reshape(-1), jnp.where(live, cols_list, grid).reshape(-1),
        (counts + UNROLL - 1) // UNROLL, counts, section_pos[None], core[None],
    ])
    parity = section_pos % 2
    hidden = hidden_in.reshape(M, T, 2 * half_width)
    entering = lax.dynamic_slice_in_dim(hidden, parity * half_width, half_width, 2)
    entering_grad = lax.dynamic_slice_in_dim(
        out_grad.reshape(M, T, 2 * half_width), (1 - parity) * half_width, half_width, 2
    )
    other = hidden[:, :, half_width:].astype(f32)
    square0 = jnp.where(section_pos == 0, jnp.sum(other * other, axis=-1, keepdims=True), 0.0)
    square0 = jnp.pad(square0, ((0, 0), (0, 0), (0, tile - 1)))
    weights = blocks.reshape(turns * slots, tile, tile)
    gain_rows = gains.reshape(turns * grid, 1, tile)

    def ring(part, by):
        return lax.ppermute(part, "section", [(i, (i + by) % sections) for i in range(sections)])

    table, entering, entering_grad, square0, gain_rows = lax.optimization_barrier(
        (table, entering, entering_grad, square0, gain_rows)
    )
    stores = [None, None]
    ahead, behind, saved = {}, {}, {}
    for tick in range(plan.ticks):
        prev = saved[tick - M][0] if tick >= M else None
        sent, saved[tick], stores = forward_tick(
            plan, tick, table, entering, square0, gain_rows, weights, prev,
            ahead.get(tick - LAG), behind.get(tick - plan.span), stores,
        )
        if tick + LAG < plan.ticks:
            ahead[tick] = ring(sent, 1)
        if tick + plan.span < plan.ticks:
            behind[tick] = ring(sent, -1)
    normed = stores

    swap = [(i, i ^ 1) for i in range(replicas)]
    share = slots // replicas

    def finish(turn, error):
        pairs = []
        for own in (normed[turn], error):
            other_core = lax.ppermute(own, "dp", swap)
            pairs.append([own, other_core])
        part = tile_grads(plan, turn, table, pairs[0], pairs[1], share, 2)
        groups = [[i for i in range(replicas) if i % 2 == c] for c in range(2)]
        chips = replicas // 2
        parts = lax.all_to_all(part.reshape(chips, share, tile, tile), "dp", 0, 0, axis_index_groups=groups, tiled=True)
        return sum_parts(parts)

    stores = [None, None]
    ahead, behind, grads = {}, {}, {}
    results = [None] * turns
    for back in range(plan.ticks):
        tick = plan.ticks - 1 - back
        sent, grads[back], stores = backward_tick(
            plan, tick, table, entering_grad, gain_rows, weights, saved[tick], grads.get(back - M),
            ahead.get(back - LAG), behind.get(back - plan.span), stores,
        )
        if back + LAG < plan.ticks:
            ahead[back] = ring(sent, -1)
        if back + plan.span < plan.ticks:
            behind[back] = ring(sent, 1)
        if back == M + plan.span - 1:
            results[1] = finish(1, stores[1])
    results[0] = finish(0, stores[0])
    return jnp.stack(results)[:, None]


def solution(mesh):
    return jax.shard_map(
        body,
        mesh=mesh,
        in_specs=(
            P(None, "dp", None),
            P(None, "dp", None),
            P(None, "section", None),
            P(None, "section", None, None, None),
            P(None, "section", None),
            P(None, "section", None),
            P(None, "section"),
        ),
        out_specs=P(None, "section", "dp", None, None),
        check_vma=False,
    )
```

```python
import jax
import jax.numpy as jnp
from jax import lax
from jax.experimental import pallas as pl
from jax.experimental.pallas import tpu as pltpu
from jax.sharding import PartitionSpec as P

norm_eps = 1e-05
LAG = 1
UNROLL = 32
STEP = 8
FLIP = 8
f32 = jnp.float32
bf16 = jnp.bfloat16
VM = pl.BlockSpec(memory_space=pltpu.VMEM)
SM = pl.BlockSpec(memory_space=pltpu.SMEM)
HBM = pl.BlockSpec(memory_space=pltpu.HBM)
LIMIT = 10 * 2**20
GRAD_LIMIT = 12 * 2**20


def split_pair(value, width):
    high = value.astype(bf16).astype(f32)
    low = value - high
    lane = lax.broadcasted_iota(jnp.int32, (value.shape[0], width), 1)
    return jnp.where(lane == 0, high, jnp.where(lane == 1, low, 0.0)).astype(bf16)


def tile_loop(gather_from, scatter_to, first, live, trash, source, weights, offset, acc):
    def group(g, carry):
        for k in range(UNROLL):
            n = g * UNROLL + k
            put = jnp.where(n < live, scatter_to[first + n], trash)
            acc[put] += jnp.dot(source[gather_from[first + n]], weights[offset + n], preferred_element_type=f32)
        return carry

    lax.fori_loop(0, (live + UNROLL - 1) // UNROLL, group, 0)


def each_block(count, visit, carry=0):
    def step(i, carry):
        for k in range(STEP):
            carry = visit(i * STEP + k, carry)
        return carry

    return lax.fori_loop(0, count // STEP, step, carry)


class Plan:
    def __init__(self, sections, turns, slots, tile, grid, tokens):
        self.sections, self.turns, self.slots = sections, turns, slots
        self.tile, self.grid = tile, grid
        self.units = sections * LAG
        self.rows = tokens // self.units
        self.span = (sections - 1) * LAG
        self.bundle = 2 * LAG
        self.ticks = turns * self.units + self.span
        self.section, self.half = turns, turns + 1

    def piece(self, dtype, extra=0):
        return jax.ShapeDtypeStruct((self.grid + extra, self.rows, self.tile), dtype)


def lane_sum(value):
    return jnp.sum(value.astype(f32), axis=-1, keepdims=True)


def tick_call(plan, tick, order, forward, named, stores, pack, turned, last):
    G, T, B, M = plan.grid, plan.rows, plan.tile, plan.units
    width = 2 * G * B
    named = {name: value for name, value in named.items() if value is not None}
    names = list(named)
    use_entering, use_prev = "entering" in named, "prev" in named
    first_turn = 0 if forward else 1
    turns_here = [first_turn] * use_entering + [1 - first_turn] * use_prev
    critical, early = "critical" in named, "early" in named
    early_at = (order - plan.span) % plan.bundle
    saves = ["kept", "slope", "scale"] if forward else ["grad"]
    piece = tick if tick < plan.span else tick - plan.turns * M
    turning = forward and (tick < plan.span or tick >= plan.turns * M)
    share = FLIP * -(-plan.slots // (plan.span * FLIP))
    piece_size = min(share, plan.slots - share * piece) if turning else 0

    shapes = {"sent": (VM, plan.piece(bf16, 1))}
    for name in saves:
        shape, kind = ((T, B), f32) if name == "scale" else ((G, T, B), bf16)
        shapes[name + "_out"] = (HBM, jax.ShapeDtypeStruct(shape, kind) if last else pltpu.HBM(shape, kind))
    alias_from = {}
    for turn in turns_here:
        shapes["store%d" % turn] = (HBM, pltpu.HBM((M, G, T, B), bf16))
        if stores[turn] is not None:
            alias_from["store%d" % turn] = stores[turn]
    if turning:
        for turn in range(2):
            shapes["turned%d" % turn] = (HBM, pltpu.HBM((plan.slots, B, B), bf16))
            if turned[turn] is not None:
                alias_from["turned%d" % turn] = turned[turn]
    if pack:
        shapes["bundle"] = (VM, jax.ShapeDtypeStruct((plan.bundle, G, T, B), bf16))
    out_names = list(shapes)
    scratch = {"source": pltpu.VMEM((G, T, B), bf16), "acc": pltpu.VMEM((G + 1, T, B), f32)}
    for name in saves:
        scratch[name + "_new"] = pltpu.VMEM((T, B), f32) if name == "scale" else pltpu.VMEM((G, T, B), bf16)
    if turning:
        scratch["flipped"] = pltpu.VMEM((2, piece_size, B, B), bf16)
    if forward and tick < M:
        scratch["extra"] = pltpu.VMEM((T, B), f32)
    scratch["sems"] = pltpu.SemaphoreType.DMA((5,))
    if pack:
        scratch["pack_sems"] = pltpu.SemaphoreType.DMA((plan.bundle,))

    def kernel(*refs):
        ref = dict(zip(names, refs))
        rest = refs[len(names) + len(pack) + len(alias_from):]
        older_sent = refs[len(names):len(names) + len(pack)]
        out = dict(zip(out_names, rest))
        own = dict(zip(scratch, rest[len(out_names):]))
        tab, sent, acc, source, sems = ref["info"], out["sent"], own["acc"], own["source"], own["sems"]
        step = tick - LAG * tab[plan.section]
        active = (step >= 0) & (step < 2 * M)
        parity = tab[plan.section] % 2
        entry = (parity if forward else 1 - parity) * (G * B)
        packing = [pltpu.make_async_copy(old.at[pl.ds(0, G)], out["bundle"].at[i], own["pack_sems"].at[i]) for i, old in enumerate(pack and older_sent)]
        for copy in packing:
            copy.start()

        def arriving(turn, unit, b):
            if use_entering:
                value = ref["entering"][unit, :, pl.ds(pl.multiple_of(entry + b * B, B), B)].astype(f32)
            if use_prev:
                older = ref["prev"][b].astype(f32)
                value = jnp.where(turn == first_turn, value, older) if use_entering else older
            if early:
                value = value + ref["early"][early_at, b].astype(f32)
            if critical:
                value = value + ref["critical"][b].astype(f32)
            return value.astype(bf16)

        def send(b, value):
            sent[b] = value
            if pack:
                out["bundle"][plan.bundle - 1, b] = value

        def keep(turn, unit, copies):
            for place in turns_here:
                @pl.when(turn == place)
                def _():
                    pltpu.make_async_copy(source, out["store%d" % place].at[unit], sems.at[0]).start()
            for copy in copies:
                copy.start()
            acc[...] = jnp.zeros_like(acc)

        def multiply(turn):
            live = tab[turn]
            gather_from, scatter_to = (ref["rows"], ref["cols"]) if forward else (ref["cols"], ref["rows"])
            if forward:
                tile_loop(gather_from, scatter_to, turn * plan.slots, live, G, source, ref["weights"], turn * plan.slots, acc)
            for place in turns_here * (not forward):
                @pl.when(turn == place)
                def _():
                    tile_loop(gather_from, scatter_to, place * plan.slots, live, G, source, ref["weights%d" % place], 0, acc)

        @pl.when(active)
        def _():
            turn = jnp.where(step >= M, 1, 0)
            unit = step - turn * M

            def gain(b):
                return ref["gains"][turn * G + b]

            if forward:
                kept, slope, scale = own["kept_new"], own["slope_new"], own["scale_new"]

                def enter(b, squares):
                    value = arriving(turn, unit, b)
                    kept[b] = value
                    value = value.astype(f32)
                    return squares + value * value

                square = lane_sum(each_block(G, enter, jnp.zeros((T, B), f32)))
                total = square
                if critical:
                    total = total + lane_sum(ref["critical"][G])
                if tick < M:
                    extra = own["extra"]
                    extra[...] = jnp.zeros_like(extra)

                    @pl.when(tab[plan.section] == 0)
                    def _():
                        def other(b, squares):
                            value = ref["entering"][unit, :, pl.ds(pl.multiple_of((G + b) * B, B), B)].astype(f32)
                            return squares + value * value

                        extra[...] = each_block(G, other, jnp.zeros((T, B), f32))

                    total = total + lane_sum(extra[...])
                inv_rms = lax.rsqrt(total / width + norm_eps)
                scale[...] = jnp.broadcast_to(inv_rms, (T, B))

                def normalize(b, carry):
                    source[b] = (kept[b].astype(f32) * inv_rms * gain(b)).astype(bf16)
                    return carry

                each_block(G, normalize)
                copies = [pltpu.make_async_copy(kept, out["kept_out"], sems.at[1]),
                          pltpu.make_async_copy(scale, out["scale_out"], sems.at[2])]
                keep(turn, unit, copies)
                multiply(turn)

                def activate(b, carry):
                    mixed = acc[b]
                    gate = jax.nn.sigmoid(mixed)
                    send(b, (mixed * gate).astype(bf16))
                    slope[b] = (gate * (1.0 + mixed * (1.0 - gate))).astype(bf16)
                    return carry

                half = G // 2
                for part in range(2):
                    each_block(half, lambda b, carry: activate(part * half + b, carry))
                    where = pl.ds(part * half, half)
                    copies.append(pltpu.make_async_copy(slope.at[where], out["slope_out"].at[where], sems.at[3 + part]))
                    copies[-1].start()
                sent[G] = split_pair(square, B)
            else:
                grad = own["grad_new"]

                def enter(b, carry):
                    value = arriving(turn, unit, b)
                    grad[b] = value
                    source[b] = (value.astype(f32) * ref["slope"][b].astype(f32)).astype(bf16)
                    return carry

                each_block(G, enter)
                copies = [pltpu.make_async_copy(grad, out["grad_out"], sems.at[1])]
                keep(turn, unit, copies)
                multiply(turn)

                def weigh(b, inner):
                    weighted = acc[b] * gain(b)
                    acc[b] = weighted
                    return inner + weighted * ref["kept"][b].astype(f32)

                inner = lane_sum(each_block(G, weigh, jnp.zeros((T, B), f32)))
                inv_rms = ref["scale"][:, 0:1]
                factor = inv_rms * inv_rms * inv_rms / width * inner
                total = factor
                if critical:
                    total = total + lane_sum(ref["critical"][G])

                def leave(b, carry):
                    send(b, (inv_rms * acc[b] - total * ref["kept"][b].astype(f32)).astype(bf16))
                    return carry

                each_block(G, leave)
                sent[G] = split_pair(factor, B)
            pltpu.make_async_copy(source, out["store%d" % turns_here[0]].at[unit], sems.at[0]).wait()
            for copy in copies:
                copy.wait()

        @pl.when(jnp.logical_not(active))
        def _():
            sent[...] = jnp.zeros_like(sent)
            if pack:
                out["bundle"][plan.bundle - 1] = jnp.zeros((G, T, B), bf16)
            if turning:
                flipped = own["flipped"]
                moves = []
                for place in range(2):

                    def flip(i, carry):
                        for k in range(FLIP):
                            at = i * FLIP + k
                            flipped[place, at] = ref["weights"][place * plan.slots + piece * share + at].T
                        return carry

                    lax.fori_loop(0, piece_size // FLIP, flip, 0)
                    moves.append(pltpu.make_async_copy(
                        flipped.at[place], out["turned%d" % place].at[pl.ds(piece * share, piece_size)], sems.at[place]))
                    moves[-1].start()
                for copy in moves:
                    copy.wait()

        for copy in packing:
            copy.wait()

    ins = list(named.values()) + list(pack) + list(alias_from.values())
    outs = pl.pallas_call(
        kernel,
        in_specs=[SM] * 3 + [VM] * (len(names) - 3 + len(pack)) + [HBM] * len(alias_from),
        out_specs=[spec for spec, _ in shapes.values()],
        out_shape=[shape for _, shape in shapes.values()],
        input_output_aliases={len(names) + len(pack) + i: out_names.index(name) for i, name in enumerate(alias_from)},
        scratch_shapes=list(scratch.values()),
        compiler_params=pltpu.CompilerParams(vmem_limit_bytes=LIMIT),
        name="forward_tick" if forward else "backward_tick",
    )(*ins)
    return dict(zip(out_names, outs))


def tile_grads(plan, turn, info, rows, cols, normed_pair, error_pair, share, parts):
    G, T, B, M = plan.grid, plan.rows, plan.tile, plan.units
    local = plan.slots // parts
    steps = 8
    chunk = local // steps
    tokens = M * T

    def kernel(tab, rows_at, cols_at, *refs):
        normeds, errors = refs[:parts], refs[parts:2 * parts]
        out, turned, flat = refs[2 * parts:]
        step = pl.program_id(0)

        @pl.when(step == 0)
        def _():
            for b in range(G):
                for p in range(parts):
                    for m in range(M):
                        at = p * tokens + m * T
                        flat[b, at:at + T, :] = errors[p][m, b]
                    whole = jnp.concatenate([normeds[p][m, b] for m in range(M)], axis=0)
                    turned[b, :, p * tokens:(p + 1) * tokens] = whole.T

        half = tab[plan.half]
        live = tab[turn]
        for k in range(chunk):
            i = step * chunk + k
            n = (i // share) * (share * parts) + half * share + i % share
            at = turn * plan.slots + n
            made = jnp.dot(turned[rows_at[at]], flat[cols_at[at]], preferred_element_type=f32)
            out[k] = jnp.where(n < live, made, 0.0).astype(bf16)

    whole = pl.BlockSpec((M, G, T, B), lambda i, *_: (0, 0, 0, 0))
    return pl.pallas_call(
        kernel,
        grid_spec=pltpu.PrefetchScalarGridSpec(
            num_scalar_prefetch=3,
            grid=(steps,),
            in_specs=[whole] * (2 * parts),
            out_specs=pl.BlockSpec((chunk, B, B), lambda i, *_: (i, 0, 0)),
            scratch_shapes=[pltpu.VMEM((G, B, parts * tokens), bf16), pltpu.VMEM((G, parts * tokens, B), bf16)],
        ),
        out_shape=pltpu.HBM((local, B, B), bf16),
        compiler_params=pltpu.CompilerParams(vmem_limit_bytes=GRAD_LIMIT),
        cost_estimate=pl.CostEstimate(flops=2 * local * B * B * parts * tokens, transcendentals=0, bytes_accessed=24 * 2**20),
        name="tile_grads",
    )(info, rows, cols, *normed_pair, *error_pair)


def sum_parts(parts):
    def kernel(given, out):
        total = given[0].astype(f32)
        for i in range(1, parts.shape[0]):
            total = total + given[i].astype(f32)
        out[...] = total.astype(bf16)

    rest = parts.shape[2:]
    return pl.pallas_call(
        kernel,
        grid=(parts.shape[1] // 2,),
        in_specs=[pl.BlockSpec((parts.shape[0], 2, *rest), lambda i: (0, i, 0, 0))],
        out_specs=pl.BlockSpec((2, *rest), lambda i: (i, 0, 0)),
        out_shape=jax.ShapeDtypeStruct(parts.shape[1:], bf16),
        compiler_params=pltpu.CompilerParams(vmem_limit_bytes=GRAD_LIMIT),
        name="sum_parts",
    )(parts)


def body(hidden_in, out_grad, gains, blocks, block_rows, block_cols, block_counts):
    sections = lax.axis_size("section")
    replicas = lax.axis_size("dp")
    section_pos = lax.axis_index("section").astype(jnp.int32)
    core = (lax.axis_index("dp") % 2).astype(jnp.int32)
    turns, slots, tile = blocks.shape[0], blocks.shape[2], blocks.shape[3]
    tokens = hidden_in.shape[0] * hidden_in.shape[1]
    half_width = hidden_in.shape[2] // 2
    grid = half_width // tile
    plan = Plan(sections, turns, slots, tile, grid, tokens)
    M, T = plan.units, plan.rows

    rows, cols = block_rows.reshape(-1), block_cols.reshape(-1)
    info = jnp.concatenate([block_counts.reshape(-1), section_pos[None], core[None]])
    entering = hidden_in.reshape(M, T, 2 * half_width)
    entering_grad = out_grad.reshape(M, T, 2 * half_width)
    weights = blocks.reshape(turns * slots, tile, tile)
    gain_rows = gains.reshape(turns * grid, 1, tile)

    def ring(part, by):
        return lax.ppermute(part, "section", [(i, (i + by) % sections) for i in range(sections)])

    def run(forward, weights, saved, hook):
        stores, turned = [None, None], [None, None]
        sents, ahead, bundles, kept = [], [], {}, []
        toward = 1 if forward else -1
        for order in range(plan.ticks):
            tick = order if forward else plan.ticks - 1 - order
            use_entering, use_prev = order < M + plan.span, order >= M
            named = dict(info=info, rows=rows, cols=cols, gains=gain_rows)
            if forward:
                named["weights"] = weights
            else:
                named["weights1"] = weights[1] if use_entering else None
                named["weights0"] = weights[0] if use_prev else None
            named["entering"] = (entering if forward else entering_grad) if use_entering else None
            if forward:
                named["prev"] = kept[order - M]["kept_out"] if use_prev else None
            else:
                named["kept"], named["slope"], named["scale"] = [saved[tick][name + "_out"] for name in ("kept", "slope", "scale")]
                named["prev"] = kept[order - M]["grad_out"] if use_prev else None
            named["critical"] = ahead[order - LAG] if order >= LAG else None
            named["early"] = bundles[(order - plan.span) // plan.bundle] if order >= plan.span else None
            pack = ()
            if order % plan.bundle == plan.bundle - 1 and order - plan.bundle + 1 + plan.span < plan.ticks:
                pack = tuple(sents[order - plan.bundle + 1:order])
            made = tick_call(plan, tick, order, forward, named, stores, pack, turned, order == plan.ticks - 1)
            sents.append(made["sent"])
            kept.append(made)
            stores = [made.get("store%d" % turn, stores[turn]) for turn in range(2)]
            turned = [made.get("turned%d" % turn, turned[turn]) for turn in range(2)]
            ahead.append(ring(made["sent"], toward) if order + LAG < plan.ticks else None)
            if pack:
                bundles[order // plan.bundle] = ring(made["bundle"], -toward)
            hook(order, ahead, stores)
        return kept, stores, turned

    saved, normed, turned = run(True, weights, None, lambda order, ahead, stores: None)

    chips = replicas // 2
    swap = [(i, i ^ 1) for i in range(replicas)]
    share = slots // replicas
    same_core = [[i for i in range(replicas) if i % 2 == c] for c in range(2)]

    def make_grads(turn, error):
        pairs = [[own, lax.ppermute(own, "dp", swap)] for own in (normed[turn], error)]
        return tile_grads(plan, turn, info, rows, cols, pairs[0], pairs[1], share, 2)

    def trade(part):
        return lax.all_to_all(
            part.reshape(chips, share, tile, tile), "dp", 0, 0, axis_index_groups=same_core, tiled=True
        )

    later = []

    def halfway(order, ahead, stores):
        if order == M + plan.span - 1:
            part, ahead[order] = lax.optimization_barrier((make_grads(1, stores[1]), ahead[order]))
            later.append(trade(part))

    _, errors, _ = run(False, turned, saved, halfway)
    sooner = trade(make_grads(0, errors[0]))
    results = [sum_parts(sooner), sum_parts(later[0])]
    return jnp.stack(results)[:, None]


def solution(mesh):
    return jax.shard_map(
        body,
        mesh=mesh,
        in_specs=(
            P(None, "dp", None),
            P(None, "dp", None),
            P(None, "section", None),
            P(None, "section", None, None, None),
            P(None, "section", None),
            P(None, "section", None),
            P(None, "section"),
        ),
        out_specs=P(None, "section", "dp", None, None),
        check_vma=False,
    )
```

```python
import jax
import jax.numpy as jnp
from jax import lax
from jax.experimental import pallas as pl
from jax.experimental.pallas import tpu as pltpu
from jax.sharding import PartitionSpec as P

norm_eps = 1e-05
LAG = 1
UNROLL = 32
STEP = 8
FLIP = 8
f32 = jnp.float32
bf16 = jnp.bfloat16
VM = pl.BlockSpec(memory_space=pltpu.VMEM)
SM = pl.BlockSpec(memory_space=pltpu.SMEM)
HBM = pl.BlockSpec(memory_space=pltpu.HBM)
LIMIT = 10 * 2**20
GRAD_LIMIT = 9 * 2**20
PARTS = 2


def split_pair(value, width):
    high = value.astype(bf16).astype(f32)
    low = value - high
    lane = lax.broadcasted_iota(jnp.int32, (value.shape[0], width), 1)
    return jnp.where(lane == 0, high, jnp.where(lane == 1, low, 0.0)).astype(bf16)


def tile_loop(gather_from, scatter_to, first, live, trash, source, weights, offset, acc):
    def group(g, carry):
        for k in range(UNROLL):
            n = g * UNROLL + k
            put = jnp.where(n < live, scatter_to[first + n], trash)
            acc[put] += jnp.dot(source[gather_from[first + n]], weights[offset + n], preferred_element_type=f32)
        return carry

    lax.fori_loop(0, (live + UNROLL - 1) // UNROLL, group, 0)


def each_block(count, visit, carry=0):
    def step(i, carry):
        for k in range(STEP):
            carry = visit(i * STEP + k, carry)
        return carry

    return lax.fori_loop(0, count // STEP, step, carry)


class Plan:
    def __init__(self, sections, turns, slots, tile, grid, tokens):
        self.sections, self.turns, self.slots = sections, turns, slots
        self.tile, self.grid = tile, grid
        self.units = sections * LAG
        self.rows = tokens // self.units
        self.span = (sections - 1) * LAG
        self.bundle = 2 * LAG
        self.ticks = turns * self.units + self.span
        self.section, self.half = turns, turns + 1

    def piece(self, dtype, extra=0):
        return jax.ShapeDtypeStruct((self.grid + extra, self.rows, self.tile), dtype)


def lane_sum(value):
    return jnp.sum(value.astype(f32), axis=-1, keepdims=True)


def tick_call(plan, tick, order, forward, named, stores, pack, turned, last):
    G, T, B, M = plan.grid, plan.rows, plan.tile, plan.units
    width = 2 * G * B
    named = {name: value for name, value in named.items() if value is not None}
    names = list(named)
    use_entering, use_prev = "entering" in named, "prev" in named
    first_turn = 0 if forward else 1
    turns_here = [first_turn] * use_entering + [1 - first_turn] * use_prev
    critical, early = "critical" in named, "early" in named
    early_at = (order - plan.span - 1) % plan.bundle
    saves = ["kept", "slope", "scale"] if forward else ["grad"]
    piece = tick if tick < plan.span else tick - plan.turns * M
    turning = forward and (tick < plan.span or tick >= plan.turns * M)
    share = FLIP * -(-plan.slots // (plan.span * FLIP))
    piece_size = min(share, plan.slots - share * piece) if turning else 0

    shapes = {"sent": (VM, plan.piece(bf16, 1))}
    for name in saves:
        shape, kind = ((T, B), f32) if name == "scale" else ((G, T, B), bf16)
        shapes[name + "_out"] = (HBM, jax.ShapeDtypeStruct(shape, kind) if last else pltpu.HBM(shape, kind))
    alias_from = {}
    slots_of = ["store%d" % turn for turn in turns_here]
    for name in slots_of:
        shapes[name] = (HBM, pltpu.HBM((M, G, T, B), bf16))
        if name in stores:
            alias_from[name] = stores[name]
    if turning:
        for turn in range(2):
            shapes["turned%d" % turn] = (HBM, pltpu.HBM((plan.slots, B, B), bf16))
            if turned[turn] is not None:
                alias_from["turned%d" % turn] = turned[turn]
    packs = pack is not None
    pack = pack or ()
    if packs:
        shapes["bundle"] = (VM, jax.ShapeDtypeStruct((plan.bundle, G, T, B), bf16))
    out_names = list(shapes)
    scratch = {"source": pltpu.VMEM((G, T, B), bf16), "acc": pltpu.VMEM((G + 1, T, B), f32)}
    for name in saves:
        scratch[name + "_new"] = pltpu.VMEM((T, B), f32) if name == "scale" else pltpu.VMEM((G, T, B), bf16)
    if turning:
        scratch["flipped"] = pltpu.VMEM((2, piece_size, B, B), bf16)
    if forward and tick < M:
        scratch["extra"] = pltpu.VMEM((T, B), f32)
    scratch["sems"] = pltpu.SemaphoreType.DMA((5,))
    if packs:
        scratch["pack_sems"] = pltpu.SemaphoreType.DMA((plan.bundle,))

    def kernel(*refs):
        ref = dict(zip(names, refs))
        rest = refs[len(names) + len(pack) + len(alias_from):]
        older_sent = refs[len(names):len(names) + len(pack)]
        out = dict(zip(out_names, rest))
        own = dict(zip(scratch, rest[len(out_names):]))
        tab, sent, acc, source, sems = ref["info"], out["sent"], own["acc"], own["source"], own["sems"]
        step = tick - LAG * tab[plan.section]
        active = (step >= 0) & (step < 2 * M)
        parity = tab[plan.section] % 2
        entry = (parity if forward else 1 - parity) * (G * B)
        packing = [pltpu.make_async_copy(old.at[pl.ds(0, G)], out["bundle"].at[i], own["pack_sems"].at[i]) for i, old in enumerate(older_sent)]
        for copy in packing:
            copy.start()

        def arriving(turn, unit, b):
            if use_entering:
                value = ref["entering"][unit, :, pl.ds(pl.multiple_of(entry + b * B, B), B)].astype(f32)
            if use_prev:
                older = ref["prev"][b].astype(f32)
                value = jnp.where(turn == first_turn, value, older) if use_entering else older
            if early:
                value = value + ref["early"][early_at, b].astype(f32)
            if critical:
                value = value + ref["critical"][b].astype(f32)
            return value.astype(bf16)

        def send(b, value):
            sent[b] = value
            if packs:
                out["bundle"][plan.bundle - 1, b] = value

        def keep(turn, unit, copies):
            for place, name in zip(turns_here, slots_of):
                @pl.when(turn == place)
                def _():
                    pltpu.make_async_copy(source, out[name].at[unit], sems.at[0]).start()
            for copy in copies:
                copy.start()
            acc[...] = jnp.zeros_like(acc)

        def multiply(turn):
            live = tab[turn]
            gather_from, scatter_to = (ref["rows"], ref["cols"]) if forward else (ref["cols"], ref["rows"])
            if forward:
                tile_loop(gather_from, scatter_to, turn * plan.slots, live, G, source, ref["weights"], turn * plan.slots, acc)
            for place in turns_here * (not forward):
                @pl.when(turn == place)
                def _():
                    tile_loop(gather_from, scatter_to, place * plan.slots, live, G, source, ref["weights%d" % place], 0, acc)

        @pl.when(active)
        def _():
            turn = jnp.where(step >= M, 1, 0)
            unit = step - turn * M

            def gain(b):
                return ref["gains"][turn * G + b]

            if forward:
                kept, slope, scale = own["kept_new"], own["slope_new"], own["scale_new"]

                def enter(b, squares):
                    value = arriving(turn, unit, b)
                    kept[b] = value
                    value = value.astype(f32)
                    return squares + value * value

                square = lane_sum(each_block(G, enter, jnp.zeros((T, B), f32)))
                total = square
                if critical:
                    total = total + lane_sum(ref["critical"][G])
                if tick < M:
                    extra = own["extra"]
                    extra[...] = jnp.zeros_like(extra)

                    @pl.when(tab[plan.section] == 0)
                    def _():
                        def other(b, squares):
                            value = ref["entering"][unit, :, pl.ds(pl.multiple_of((G + b) * B, B), B)].astype(f32)
                            return squares + value * value

                        extra[...] = each_block(G, other, jnp.zeros((T, B), f32))

                    total = total + lane_sum(extra[...])
                inv_rms = lax.rsqrt(total / width + norm_eps)
                scale[...] = jnp.broadcast_to(inv_rms, (T, B))

                def normalize(b, carry):
                    source[b] = (kept[b].astype(f32) * inv_rms * gain(b)).astype(bf16)
                    return carry

                each_block(G, normalize)
                copies = [pltpu.make_async_copy(kept, out["kept_out"], sems.at[1]),
                          pltpu.make_async_copy(scale, out["scale_out"], sems.at[2])]
                keep(turn, unit, copies)
                multiply(turn)

                def activate(b, carry):
                    mixed = acc[b]
                    gate = jax.nn.sigmoid(mixed)
                    send(b, (mixed * gate).astype(bf16))
                    slope[b] = (gate * (1.0 + mixed * (1.0 - gate))).astype(bf16)
                    return carry

                half = G // 2
                for part in range(2):
                    each_block(half, lambda b, carry: activate(part * half + b, carry))
                    where = pl.ds(part * half, half)
                    copies.append(pltpu.make_async_copy(slope.at[where], out["slope_out"].at[where], sems.at[3 + part]))
                    copies[-1].start()
                sent[G] = split_pair(square, B)
            else:
                grad = own["grad_new"]

                def enter(b, carry):
                    value = arriving(turn, unit, b)
                    grad[b] = value
                    source[b] = (value.astype(f32) * ref["slope"][b].astype(f32)).astype(bf16)
                    return carry

                each_block(G, enter)
                copies = [pltpu.make_async_copy(grad, out["grad_out"], sems.at[1])]
                keep(turn, unit, copies)
                multiply(turn)

                def weigh(b, inner):
                    weighted = acc[b] * gain(b)
                    acc[b] = weighted
                    return inner + weighted * ref["kept"][b].astype(f32)

                inner = lane_sum(each_block(G, weigh, jnp.zeros((T, B), f32)))
                inv_rms = ref["scale"][:, 0:1]
                factor = inv_rms * inv_rms * inv_rms / width * inner
                total = factor
                if critical:
                    total = total + lane_sum(ref["critical"][G])

                def leave(b, carry):
                    send(b, (inv_rms * acc[b] - total * ref["kept"][b].astype(f32)).astype(bf16))
                    return carry

                each_block(G, leave)
                sent[G] = split_pair(factor, B)
            pltpu.make_async_copy(source, out[slots_of[0]].at[unit], sems.at[0]).wait()
            for copy in copies:
                copy.wait()

        @pl.when(jnp.logical_not(active))
        def _():
            sent[...] = jnp.zeros_like(sent)
            if packs:
                out["bundle"][plan.bundle - 1] = jnp.zeros((G, T, B), bf16)
            if turning:
                flipped = own["flipped"]
                moves = []
                for place in range(2):

                    def flip(i, carry):
                        for k in range(FLIP):
                            at = i * FLIP + k
                            flipped[place, at] = ref["weights"][place * plan.slots + piece * share + at].T
                        return carry

                    lax.fori_loop(0, piece_size // FLIP, flip, 0)
                    moves.append(pltpu.make_async_copy(
                        flipped.at[place], out["turned%d" % place].at[pl.ds(piece * share, piece_size)], sems.at[place]))
                    moves[-1].start()
                for copy in moves:
                    copy.wait()

        for copy in packing:
            copy.wait()

    ins = list(named.values()) + list(pack) + list(alias_from.values())
    outs = pl.pallas_call(
        kernel,
        in_specs=[SM] * 3 + [VM] * (len(names) - 3 + len(pack)) + [HBM] * len(alias_from),
        out_specs=[spec for spec, _ in shapes.values()],
        out_shape=[shape for _, shape in shapes.values()],
        input_output_aliases={len(names) + len(pack) + i: out_names.index(name) for i, name in enumerate(alias_from)},
        scratch_shapes=list(scratch.values()),
        compiler_params=pltpu.CompilerParams(vmem_limit_bytes=LIMIT),
        name="forward_tick" if forward else "backward_tick",
    )(*ins)
    return dict(zip(out_names, outs))


def tile_grads(plan, turn, info, rows, cols, normed_parts, error_parts, share, parts):
    G, T, B, M = plan.grid, plan.rows, plan.tile, plan.units
    local = plan.slots // parts
    steps = 8
    chunk = local // steps
    tokens = M * T

    def kernel(tab, rows_at, cols_at, *refs):
        normeds, errors = refs[:parts], refs[parts:2 * parts]
        out, turned, flat = refs[-3:]
        step = pl.program_id(0)

        @pl.when(step == 0)
        def _():
            for b in range(G):
                for p in range(parts):
                    for m in range(M):
                        at = p * tokens + m * T
                        flat[b, at:at + T, :] = errors[p][m, b]
                    whole = jnp.concatenate([normeds[p][m, b] for m in range(M)], axis=0)
                    turned[b, :, p * tokens:(p + 1) * tokens] = whole.T

        half = tab[plan.half]
        live = tab[turn]
        for k in range(chunk):
            i = step * chunk + k
            n = (i // share) * (share * parts) + half * share + i % share
            at = turn * plan.slots + n
            made = jnp.dot(turned[rows_at[at]], flat[cols_at[at]], preferred_element_type=f32)
            out[k] = jnp.where(n < live, made, 0.0).astype(bf16)

    whole = pl.BlockSpec((M, G, T, B), lambda i, *_: (0, 0, 0, 0))
    return pl.pallas_call(
        kernel,
        grid_spec=pltpu.PrefetchScalarGridSpec(
            num_scalar_prefetch=3,
            grid=(steps,),
            in_specs=[whole] * (2 * parts),
            out_specs=pl.BlockSpec((chunk, B, B), lambda i, *_: (i, 0, 0)),
            scratch_shapes=[pltpu.VMEM((G, B, parts * tokens), bf16), pltpu.VMEM((G, parts * tokens, B), bf16)],
        ),
        out_shape=pltpu.HBM((local, B, B), bf16),
        compiler_params=pltpu.CompilerParams(vmem_limit_bytes=GRAD_LIMIT),
        cost_estimate=pl.CostEstimate(flops=2 * local * B * B * parts * tokens, transcendentals=0, bytes_accessed=24 * 2**20),
        name="tile_grads",
    )(info, rows, cols, *normed_parts, *error_parts)


def sum_parts(parts):
    def kernel(given, out):
        total = given[0].astype(f32)
        for i in range(1, parts.shape[0]):
            total = total + given[i].astype(f32)
        out[...] = total.astype(bf16)

    rest = parts.shape[2:]
    return pl.pallas_call(
        kernel,
        grid=(parts.shape[1],),
        in_specs=[pl.BlockSpec((parts.shape[0], 1, *rest), lambda i: (0, i, 0, 0))],
        out_specs=pl.BlockSpec((1, *rest), lambda i: (i, 0, 0)),
        out_shape=jax.ShapeDtypeStruct(parts.shape[1:], bf16),
        compiler_params=pltpu.CompilerParams(vmem_limit_bytes=GRAD_LIMIT),
        name="sum_parts",
    )(parts)


def body(hidden_in, out_grad, gains, blocks, block_rows, block_cols, block_counts):
    sections = lax.axis_size("section")
    replicas = lax.axis_size("dp")
    section_pos = lax.axis_index("section").astype(jnp.int32)
    core = (lax.axis_index("dp") % PARTS).astype(jnp.int32)
    turns, slots, tile = blocks.shape[0], blocks.shape[2], blocks.shape[3]
    tokens = hidden_in.shape[0] * hidden_in.shape[1]
    half_width = hidden_in.shape[2] // 2
    grid = half_width // tile
    plan = Plan(sections, turns, slots, tile, grid, tokens)
    M, T = plan.units, plan.rows

    rows, cols = block_rows.reshape(-1), block_cols.reshape(-1)
    info = jnp.concatenate([block_counts.reshape(-1), section_pos[None], core[None]])
    entering = hidden_in.reshape(M, T, 2 * half_width)
    entering_grad = out_grad.reshape(M, T, 2 * half_width)
    weights = blocks.reshape(turns * slots, tile, tile)
    gain_rows = gains.reshape(turns * grid, 1, tile)

    def ring(part, by):
        return lax.ppermute(part, "section", [(i, (i + by) % sections) for i in range(sections)])

    def run(forward, weights, saved, hook):
        stores, turned = {}, [None, None]
        sents, ahead, bundles, kept = [], [], {}, []
        toward = 1 if forward else -1
        for order in range(plan.ticks):
            tick = order if forward else plan.ticks - 1 - order
            use_entering, use_prev = order < M + plan.span, order >= M
            named = dict(info=info, rows=rows, cols=cols, gains=gain_rows)
            if forward:
                named["weights"] = weights
            else:
                named["weights1"] = weights[1] if use_entering else None
                named["weights0"] = weights[0] if use_prev else None
            named["entering"] = (entering if forward else entering_grad) if use_entering else None
            if forward:
                named["prev"] = kept[order - M]["kept_out"] if use_prev else None
            else:
                named["kept"], named["slope"], named["scale"] = [saved[tick][name + "_out"] for name in ("kept", "slope", "scale")]
                named["prev"] = kept[order - M]["grad_out"] if use_prev else None
            named["critical"] = ahead[order - LAG] if order >= LAG else None
            named["early"] = bundles[-(-(order - plan.span) // plan.bundle)] if order >= plan.span else None
            pack = None
            if order % plan.bundle == 0 and order - plan.bundle + 1 + plan.span < plan.ticks:
                pack = tuple(sents[max(order - plan.bundle + 1, 0):order])
            made = tick_call(plan, tick, order, forward, named, stores, pack, turned, order == plan.ticks - 1)
            sents.append(made["sent"])
            kept.append(made)
            stores = stores | {name: made[name] for name in ("store0", "store1") if name in made}
            turned = [made.get("turned%d" % turn, turned[turn]) for turn in range(2)]
            ahead.append(ring(made["sent"], toward) if order + LAG < plan.ticks else None)
            if pack is not None:
                bundles[order // plan.bundle] = ring(made["bundle"], -toward)
            hook(order, ahead, stores)
        return kept, stores, turned

    saved, normed, turned = run(True, weights, None, lambda order, ahead, stores: None)

    members = replicas // PARTS
    share = slots // replicas
    alike = [[i for i in range(replicas) if i % PARTS == q] for q in range(PARTS)]

    def gather(own):
        return [own, lax.ppermute(own, "dp", [(i, i ^ 1) for i in range(replicas)])]

    def make_grads(turn, stores):
        name = "store%d" % turn
        return tile_grads(plan, turn, info, rows, cols, gather(normed[name]), gather(stores[name]), share, PARTS)

    def trade(part):
        return lax.all_to_all(
            part.reshape(members, share, tile, tile), "dp", 0, 0, axis_index_groups=alike, tiled=True
        )

    later = []

    def halfway(order, ahead, stores):
        if order == M + plan.span - 1:
            part, ahead[order] = lax.optimization_barrier((make_grads(1, stores), ahead[order]))
            later.append(lax.psum_scatter(part, "dp", scatter_dimension=0, axis_index_groups=alike, tiled=True))

    _, errors, _ = run(False, turned, saved, halfway)
    sooner = trade(make_grads(0, errors))
    return jnp.stack([sum_parts(sooner), later[0]])[:, None]


def solution(mesh):
    return jax.shard_map(
        body,
        mesh=mesh,
        in_specs=(
            P(None, "dp", None),
            P(None, "dp", None),
            P(None, "section", None),
            P(None, "section", None, None, None),
            P(None, "section", None),
            P(None, "section", None),
            P(None, "section"),
        ),
        out_specs=P(None, "section", "dp", None, None),
        check_vma=False,
    )
```

```python
import jax
import jax.numpy as jnp
from jax import lax
from jax.experimental import pallas as pl
from jax.experimental.pallas import tpu as pltpu
from jax.sharding import PartitionSpec as P

norm_eps = 1e-05
LAG = 1
UNROLL = 32
STEP = 8
FLIP = 8
f32 = jnp.float32
bf16 = jnp.bfloat16
VM = pl.BlockSpec(memory_space=pltpu.VMEM)
SM = pl.BlockSpec(memory_space=pltpu.SMEM)
HBM = pl.BlockSpec(memory_space=pltpu.HBM)
LIMIT = 10 * 2**20
GRAD_LIMIT = 9 * 2**20
PARTS = 2


def split_pair(value, width):
    high = value.astype(bf16).astype(f32)
    low = value - high
    lane = lax.broadcasted_iota(jnp.int32, (value.shape[0], width), 1)
    return jnp.where(lane == 0, high, jnp.where(lane == 1, low, 0.0)).astype(bf16)


def tile_loop(table, gather_at, scatter_at, live, trash, source, weights, offset, acc):
    def group(g, carry):
        for k in range(UNROLL):
            n = g * UNROLL + k
            put = jnp.where(n < live, table[scatter_at + n], trash)
            acc[put] += jnp.dot(source[table[gather_at + n]], weights[offset + n], preferred_element_type=f32)
        return carry

    lax.fori_loop(0, (live + UNROLL - 1) // UNROLL, group, 0)


def each_block(count, visit, carry=0):
    def step(i, carry):
        for k in range(STEP):
            carry = visit(i * STEP + k, carry)
        return carry

    return lax.fori_loop(0, count // STEP, step, carry)


class Plan:
    def __init__(self, sections, turns, slots, tile, grid, tokens):
        self.sections, self.turns, self.slots = sections, turns, slots
        self.tile, self.grid = tile, grid
        self.units = sections * LAG
        self.rows = tokens // self.units
        self.span = (sections - 1) * LAG
        self.bundle = 2 * LAG
        self.ticks = turns * self.units + self.span
        self.section, self.half = turns, turns + 1
        self.rows_at = turns + 2
        self.cols_at = self.rows_at + turns * slots

    def piece(self, dtype, extra=0):
        return jax.ShapeDtypeStruct((self.grid + extra, self.rows, self.tile), dtype)


def lane_sum(value):
    return jnp.sum(value.astype(f32), axis=-1, keepdims=True)


def tick_call(plan, tick, order, forward, named, stores, pack, turned, last):
    G, T, B, M = plan.grid, plan.rows, plan.tile, plan.units
    width = 2 * G * B
    named = {name: value for name, value in named.items() if value is not None}
    names = list(named)
    use_entering, use_prev = "entering" in named, "prev" in named
    first_turn = 0 if forward else 1
    turns_here = [first_turn] * use_entering + [1 - first_turn] * use_prev
    critical, early = "critical" in named, "early" in named
    early_at = (order - plan.span - 1) % plan.bundle
    saves = ["kept", "slope", "scale"] if forward else ["grad"]
    piece = tick if tick < plan.span else tick - plan.turns * M
    turning = forward and (tick < plan.span or tick >= plan.turns * M)
    share = FLIP * -(-plan.slots // (plan.span * FLIP))
    piece_size = min(share, plan.slots - share * piece) if turning else 0

    shapes = {"sent": (VM, plan.piece(bf16, 1))}
    for name in saves:
        shape, kind = ((T, B), f32) if name == "scale" else ((G, T, B), bf16)
        shapes[name + "_out"] = (HBM, jax.ShapeDtypeStruct(shape, kind) if last else pltpu.HBM(shape, kind))
    alias_from = {}
    slots_of = ["store%d" % turn for turn in turns_here]
    for name in slots_of:
        shapes[name] = (HBM, pltpu.HBM((M, G, T, B), bf16))
        if name in stores:
            alias_from[name] = stores[name]
    if turning:
        for turn in range(2):
            shapes["turned%d" % turn] = (HBM, pltpu.HBM((plan.slots, B, B), bf16))
            if turned[turn] is not None:
                alias_from["turned%d" % turn] = turned[turn]
    packs = pack is not None
    pack = pack or ()
    if packs:
        shapes["bundle"] = (VM, jax.ShapeDtypeStruct((plan.bundle, G, T, B), bf16))
    out_names = list(shapes)
    scratch = {"source": pltpu.VMEM((G, T, B), bf16), "acc": pltpu.VMEM((G + 1, T, B), f32)}
    for name in saves:
        scratch[name + "_new"] = pltpu.VMEM((T, B), f32) if name == "scale" else pltpu.VMEM((G, T, B), bf16)
    if turning:
        scratch["flipped"] = pltpu.VMEM((2, piece_size, B, B), bf16)
    if forward and tick < M:
        scratch["extra"] = pltpu.VMEM((T, B), f32)
    scratch["sems"] = pltpu.SemaphoreType.DMA((5,))
    if packs:
        scratch["pack_sems"] = pltpu.SemaphoreType.DMA((plan.bundle,))

    def kernel(*refs):
        ref = dict(zip(names, refs))
        rest = refs[len(names) + len(pack) + len(alias_from):]
        older_sent = refs[len(names):len(names) + len(pack)]
        out = dict(zip(out_names, rest))
        own = dict(zip(scratch, rest[len(out_names):]))
        tab, sent, acc, source, sems = ref["info"], out["sent"], own["acc"], own["source"], own["sems"]
        step = tick - LAG * tab[plan.section]
        active = (step >= 0) & (step < 2 * M)
        parity = tab[plan.section] % 2
        entry = (parity if forward else 1 - parity) * (G * B)
        packing = [pltpu.make_async_copy(old.at[pl.ds(0, G)], out["bundle"].at[i], own["pack_sems"].at[i]) for i, old in enumerate(older_sent)]
        for copy in packing:
            copy.start()

        def arriving(turn, unit, b):
            if use_entering:
                value = ref["entering"][unit, :, pl.ds(pl.multiple_of(entry + b * B, B), B)].astype(f32)
            if use_prev:
                older = ref["prev"][b].astype(f32)
                value = jnp.where(turn == first_turn, value, older) if use_entering else older
            if early:
                value = value + ref["early"][early_at, b].astype(f32)
            if critical:
                value = value + ref["critical"][b].astype(f32)
            return value.astype(bf16)

        def send(b, value):
            sent[b] = value
            if packs:
                out["bundle"][plan.bundle - 1, b] = value

        def keep(turn, unit, copies):
            for place, name in zip(turns_here, slots_of):
                @pl.when(turn == place)
                def _():
                    pltpu.make_async_copy(source, out[name].at[unit], sems.at[0]).start()
            for copy in copies:
                copy.start()
            acc[...] = jnp.zeros_like(acc)

        def multiply(turn):
            live = tab[turn]
            gather_at, scatter_at = (plan.rows_at, plan.cols_at) if forward else (plan.cols_at, plan.rows_at)
            if forward:
                first = turn * plan.slots
                tile_loop(tab, gather_at + first, scatter_at + first, live, G, source, ref["weights"], first, acc)
            for place in turns_here * (not forward):
                @pl.when(turn == place)
                def _():
                    first = place * plan.slots
                    tile_loop(tab, gather_at + first, scatter_at + first, live, G, source, ref["weights%d" % place], 0, acc)

        @pl.when(active)
        def _():
            turn = jnp.where(step >= M, 1, 0)
            unit = step - turn * M

            def gain(b):
                return ref["gains"][turn * G + b]

            if forward:
                kept, slope, scale = own["kept_new"], own["slope_new"], own["scale_new"]

                def enter(b, squares):
                    value = arriving(turn, unit, b)
                    kept[b] = value
                    value = value.astype(f32)
                    return squares + value * value

                square = lane_sum(each_block(G, enter, jnp.zeros((T, B), f32)))
                total = square
                if critical:
                    total = total + lane_sum(ref["critical"][G])
                if tick < M:
                    extra = own["extra"]
                    extra[...] = jnp.zeros_like(extra)

                    @pl.when(tab[plan.section] == 0)
                    def _():
                        def other(b, squares):
                            value = ref["entering"][unit, :, pl.ds(pl.multiple_of((G + b) * B, B), B)].astype(f32)
                            return squares + value * value

                        extra[...] = each_block(G, other, jnp.zeros((T, B), f32))

                    total = total + lane_sum(extra[...])
                inv_rms = lax.rsqrt(total / width + norm_eps)
                scale[...] = jnp.broadcast_to(inv_rms, (T, B))

                def normalize(b, carry):
                    source[b] = (kept[b].astype(f32) * inv_rms * gain(b)).astype(bf16)
                    return carry

                each_block(G, normalize)
                copies = [pltpu.make_async_copy(kept, out["kept_out"], sems.at[1]),
                          pltpu.make_async_copy(scale, out["scale_out"], sems.at[2])]
                keep(turn, unit, copies)
                multiply(turn)

                def activate(b, carry):
                    mixed = acc[b]
                    gate = jax.nn.sigmoid(mixed)
                    send(b, (mixed * gate).astype(bf16))
                    slope[b] = (gate * (1.0 + mixed * (1.0 - gate))).astype(bf16)
                    return carry

                half = G // 2
                for part in range(2):
                    each_block(half, lambda b, carry: activate(part * half + b, carry))
                    where = pl.ds(part * half, half)
                    copies.append(pltpu.make_async_copy(slope.at[where], out["slope_out"].at[where], sems.at[3 + part]))
                    copies[-1].start()
                sent[G] = split_pair(square, B)
            else:
                grad = own["grad_new"]

                def enter(b, carry):
                    value = arriving(turn, unit, b)
                    grad[b] = value
                    source[b] = (value.astype(f32) * ref["slope"][b].astype(f32)).astype(bf16)
                    return carry

                each_block(G, enter)
                copies = [pltpu.make_async_copy(grad, out["grad_out"], sems.at[1])]
                keep(turn, unit, copies)
                multiply(turn)

                def weigh(b, inner):
                    weighted = acc[b] * gain(b)
                    acc[b] = weighted
                    return inner + weighted * ref["kept"][b].astype(f32)

                inner = lane_sum(each_block(G, weigh, jnp.zeros((T, B), f32)))
                inv_rms = ref["scale"][:, 0:1]
                factor = inv_rms * inv_rms * inv_rms / width * inner
                total = factor
                if critical:
                    total = total + lane_sum(ref["critical"][G])

                def leave(b, carry):
                    send(b, (inv_rms * acc[b] - total * ref["kept"][b].astype(f32)).astype(bf16))
                    return carry

                each_block(G, leave)
                sent[G] = split_pair(factor, B)
            pltpu.make_async_copy(source, out[slots_of[0]].at[unit], sems.at[0]).wait()
            for copy in copies:
                copy.wait()

        @pl.when(jnp.logical_not(active))
        def _():
            sent[...] = jnp.zeros_like(sent)
            if packs:
                out["bundle"][plan.bundle - 1] = jnp.zeros((G, T, B), bf16)
            if turning:
                flipped = own["flipped"]

                rounds = piece_size // FLIP

                def flip(i, carry):
                    place = i // rounds
                    for k in range(FLIP):
                        at = (i - place * rounds) * FLIP + k
                        flipped[place, at] = ref["weights"][place * plan.slots + piece * share + at].T
                    return carry

                lax.fori_loop(0, 2 * rounds, flip, 0)
                moves = [pltpu.make_async_copy(
                    flipped.at[place], out["turned%d" % place].at[pl.ds(piece * share, piece_size)], sems.at[place])
                    for place in range(2)]
                for copy in moves:
                    copy.start()
                for copy in moves:
                    copy.wait()

        for copy in packing:
            copy.wait()

    ins = list(named.values()) + list(pack) + list(alias_from.values())
    outs = pl.pallas_call(
        kernel,
        in_specs=[SM] + [VM] * (len(names) - 1 + len(pack)) + [HBM] * len(alias_from),
        out_specs=[spec for spec, _ in shapes.values()],
        out_shape=[shape for _, shape in shapes.values()],
        input_output_aliases={len(names) + len(pack) + i: out_names.index(name) for i, name in enumerate(alias_from)},
        scratch_shapes=list(scratch.values()),
        compiler_params=pltpu.CompilerParams(vmem_limit_bytes=LIMIT),
        name="forward_tick" if forward else "backward_tick",
    )(*ins)
    return dict(zip(out_names, outs))


def tile_grads(plan, turn, info, normed_parts, error_parts, share, parts):
    G, T, B, M = plan.grid, plan.rows, plan.tile, plan.units
    local = plan.slots // parts
    steps = 8
    chunk = local // steps
    tokens = M * T

    def kernel(tab, *refs):
        normeds, errors = refs[:parts], refs[parts:2 * parts]
        out, turned, flat = refs[-3:]
        step = pl.program_id(0)

        @pl.when(step == 0)
        def _():
            for b in range(G):
                for p in range(parts):
                    for m in range(M):
                        at = p * tokens + m * T
                        flat[b, at:at + T, :] = errors[p][m, b]
                    whole = jnp.concatenate([normeds[p][m, b] for m in range(M)], axis=0)
                    turned[b, :, p * tokens:(p + 1) * tokens] = whole.T

        half = tab[plan.half]
        live = tab[turn]
        for k in range(chunk):
            i = step * chunk + k
            n = (i // share) * (share * parts) + half * share + i % share
            at = turn * plan.slots + n
            made = jnp.dot(turned[tab[plan.rows_at + at]], flat[tab[plan.cols_at + at]], preferred_element_type=f32)
            out[k] = jnp.where(n < live, made, 0.0).astype(bf16)

    whole = pl.BlockSpec((M, G, T, B), lambda i, *_: (0, 0, 0, 0))
    return pl.pallas_call(
        kernel,
        grid_spec=pltpu.PrefetchScalarGridSpec(
            num_scalar_prefetch=1,
            grid=(steps,),
            in_specs=[whole] * (2 * parts),
            out_specs=pl.BlockSpec((chunk, B, B), lambda i, *_: (i, 0, 0)),
            scratch_shapes=[pltpu.VMEM((G, B, parts * tokens), bf16), pltpu.VMEM((G, parts * tokens, B), bf16)],
        ),
        out_shape=pltpu.HBM((local, B, B), bf16),
        compiler_params=pltpu.CompilerParams(vmem_limit_bytes=GRAD_LIMIT),
        cost_estimate=pl.CostEstimate(flops=2 * local * B * B * parts * tokens, transcendentals=0, bytes_accessed=24 * 2**20),
        name="tile_grads",
    )(info, *normed_parts, *error_parts)


def sum_parts(parts):
    def kernel(given, out):
        total = given[0].astype(f32)
        for i in range(1, parts.shape[0]):
            total = total + given[i].astype(f32)
        out[...] = total.astype(bf16)

    rest = parts.shape[2:]
    return pl.pallas_call(
        kernel,
        grid=(parts.shape[1],),
        in_specs=[pl.BlockSpec((parts.shape[0], 1, *rest), lambda i: (0, i, 0, 0))],
        out_specs=pl.BlockSpec((1, *rest), lambda i: (i, 0, 0)),
        out_shape=jax.ShapeDtypeStruct(parts.shape[1:], bf16),
        compiler_params=pltpu.CompilerParams(vmem_limit_bytes=GRAD_LIMIT),
        name="sum_parts",
    )(parts)


def body(hidden_in, out_grad, gains, blocks, block_rows, block_cols, block_counts):
    sections = lax.axis_size("section")
    replicas = lax.axis_size("dp")
    section_pos = lax.axis_index("section").astype(jnp.int32)
    core = (lax.axis_index("dp") % PARTS).astype(jnp.int32)
    turns, slots, tile = blocks.shape[0], blocks.shape[2], blocks.shape[3]
    tokens = hidden_in.shape[0] * hidden_in.shape[1]
    half_width = hidden_in.shape[2] // 2
    grid = half_width // tile
    plan = Plan(sections, turns, slots, tile, grid, tokens)
    M, T = plan.units, plan.rows

    info = jnp.concatenate(
        [block_counts.reshape(-1), section_pos[None], core[None], block_rows.reshape(-1), block_cols.reshape(-1)]
    )
    entering = hidden_in.reshape(M, T, 2 * half_width)
    entering_grad = out_grad.reshape(M, T, 2 * half_width)
    weights = blocks.reshape(turns * slots, tile, tile)
    gain_rows = gains.reshape(turns * grid, 1, tile)

    def ring(part, by):
        return lax.ppermute(part, "section", [(i, (i + by) % sections) for i in range(sections)])

    def run(forward, weights, saved, hook):
        stores, turned = {}, [None, None]
        sents, ahead, bundles, kept = [], [], {}, []
        toward = 1 if forward else -1
        for order in range(plan.ticks):
            tick = order if forward else plan.ticks - 1 - order
            use_entering, use_prev = order < M + plan.span, order >= M
            named = dict(info=info, gains=gain_rows)
            if forward:
                named["weights"] = weights
            else:
                named["weights1"] = weights[1] if use_entering else None
                named["weights0"] = weights[0] if use_prev else None
            named["entering"] = (entering if forward else entering_grad) if use_entering else None
            if forward:
                named["prev"] = kept[order - M]["kept_out"] if use_prev else None
            else:
                named["kept"], named["slope"], named["scale"] = [saved[tick][name + "_out"] for name in ("kept", "slope", "scale")]
                named["prev"] = kept[order - M]["grad_out"] if use_prev else None
            named["critical"] = ahead[order - LAG] if order >= LAG else None
            named["early"] = bundles[-(-(order - plan.span) // plan.bundle)] if order >= plan.span else None
            pack = None
            if order % plan.bundle == 0 and order - plan.bundle + 1 + plan.span < plan.ticks:
                pack = tuple(sents[max(order - plan.bundle + 1, 0):order])
            made = tick_call(plan, tick, order, forward, named, stores, pack, turned, order == plan.ticks - 1)
            sents.append(made["sent"])
            kept.append(made)
            stores = stores | {name: made[name] for name in ("store0", "store1") if name in made}
            turned = [made.get("turned%d" % turn, turned[turn]) for turn in range(2)]
            ahead.append(ring(made["sent"], toward) if order + LAG < plan.ticks else None)
            if pack is not None:
                bundles[order // plan.bundle] = ring(made["bundle"], -toward)
            hook(order, ahead, stores)
        return kept, stores, turned

    saved, normed, turned = run(True, weights, None, lambda order, ahead, stores: None)

    members = replicas // PARTS
    share = slots // replicas
    alike = [[i for i in range(replicas) if i % PARTS == q] for q in range(PARTS)]

    def gather(own):
        return [own, lax.ppermute(own, "dp", [(i, i ^ 1) for i in range(replicas)])]

    def make_grads(turn, stores):
        name = "store%d" % turn
        return tile_grads(plan, turn, info, gather(normed[name]), gather(stores[name]), share, PARTS)

    def trade(part):
        return lax.all_to_all(
            part.reshape(members, share, tile, tile), "dp", 0, 0, axis_index_groups=alike, tiled=True
        )

    later = []

    def halfway(order, ahead, stores):
        if order == M + plan.span - 1:
            part, ahead[order] = lax.optimization_barrier((make_grads(1, stores), ahead[order]))
            later.append(lax.psum_scatter(part, "dp", scatter_dimension=0, axis_index_groups=alike, tiled=True))

    _, errors, _ = run(False, turned, saved, halfway)
    sooner = trade(make_grads(0, errors))
    return jnp.stack([sum_parts(sooner), later[0]])[:, None]


def solution(mesh):
    return jax.shard_map(
        body,
        mesh=mesh,
        in_specs=(
            P(None, "dp", None),
            P(None, "dp", None),
            P(None, "section", None),
            P(None, "section", None, None, None),
            P(None, "section", None),
            P(None, "section", None),
            P(None, "section"),
        ),
        out_specs=P(None, "section", "dp", None, None),
        check_vma=False,
    )
```

```python
import jax
import jax.numpy as jnp
from jax import lax
from jax.experimental import pallas as pl
from jax.experimental.pallas import tpu as pltpu
from jax.sharding import PartitionSpec as P

norm_eps = 1e-05
LAG = 1
UNROLL = 32
STEP = 8
FLIP = 8
f32 = jnp.float32
bf16 = jnp.bfloat16
VM = pl.BlockSpec(memory_space=pltpu.VMEM)
SM = pl.BlockSpec(memory_space=pltpu.SMEM)
HBM = pl.BlockSpec(memory_space=pltpu.HBM)
LIMIT = 10 * 2**20
GRAD_LIMIT = 10 * 2**20
PARTS = 2


def split_pair(value, width):
    high = value.astype(bf16).astype(f32)
    low = value - high
    lane = lax.broadcasted_iota(jnp.int32, (value.shape[0], width), 1)
    return jnp.where(lane == 0, high, jnp.where(lane == 1, low, 0.0)).astype(bf16)


def tile_loop(table, gather_at, scatter_at, live, trash, source, weights, offset, acc):
    def group(g, carry):
        for k in range(UNROLL):
            n = g * UNROLL + k
            put = jnp.where(n < live, table[scatter_at + n], trash)
            acc[put] += jnp.dot(source[table[gather_at + n]], weights[offset + n], preferred_element_type=f32)
        return carry

    lax.fori_loop(0, (live + UNROLL - 1) // UNROLL, group, 0)


def each_block(count, visit, carry=0):
    def step(i, carry):
        for k in range(STEP):
            carry = visit(i * STEP + k, carry)
        return carry

    return lax.fori_loop(0, count // STEP, step, carry)


class Plan:
    def __init__(self, sections, turns, slots, tile, grid, tokens):
        self.sections, self.turns, self.slots = sections, turns, slots
        self.tile, self.grid = tile, grid
        self.units = sections * LAG
        self.rows = tokens // self.units
        self.span = (sections - 1) * LAG
        self.bundle = 2 * LAG
        self.ticks = turns * self.units + self.span
        self.section, self.half = turns, turns + 1
        self.rows_at = turns + 2
        self.cols_at = self.rows_at + turns * slots

    def piece(self, dtype, extra=0):
        return jax.ShapeDtypeStruct((self.grid + extra, self.rows, self.tile), dtype)


def lane_sum(value):
    return jnp.sum(value.astype(f32), axis=-1, keepdims=True)


def tick_call(plan, tick, order, forward, named, stores, pack, turned, last):
    G, T, B, M = plan.grid, plan.rows, plan.tile, plan.units
    width = 2 * G * B
    named = {name: value for name, value in named.items() if value is not None}
    names = list(named)
    use_entering, use_prev = "entering" in named, "prev" in named
    first_turn = 0 if forward else 1
    turns_here = [first_turn] * use_entering + [1 - first_turn] * use_prev
    critical, early = "critical" in named, "early" in named
    early_at = (order - plan.span - 1) % plan.bundle
    saves = ["kept", "slope", "scale"] if forward else ["grad"]
    piece = tick if tick < plan.span else tick - plan.turns * M
    turning = forward and (tick < plan.span or tick >= plan.turns * M)
    share = FLIP * -(-plan.slots // (plan.span * FLIP))
    piece_size = min(share, plan.slots - share * piece) if turning else 0

    shapes = {"sent": (VM, plan.piece(bf16, 1))}
    for name in saves:
        shape, kind = ((T, B), f32) if name == "scale" else ((G, T, B), bf16)
        shapes[name + "_out"] = (HBM, jax.ShapeDtypeStruct(shape, kind) if last else pltpu.HBM(shape, kind))
    alias_from = {}
    slots_of = ["store%d" % turn for turn in turns_here]
    for name in slots_of:
        shapes[name] = (HBM, pltpu.HBM((M, G, T, B), bf16))
        if name in stores:
            alias_from[name] = stores[name]
    if turning:
        for turn in range(2):
            shapes["turned%d" % turn] = (HBM, pltpu.HBM((plan.slots, B, B), bf16))
            if turned[turn] is not None:
                alias_from["turned%d" % turn] = turned[turn]
    packs = pack is not None
    pack = pack or ()
    if packs:
        shapes["bundle"] = (VM, jax.ShapeDtypeStruct((plan.bundle, G, T, B), bf16))
    out_names = list(shapes)
    scratch = {"source": pltpu.VMEM((G, T, B), bf16), "acc": pltpu.VMEM((G + 1, T, B), f32)}
    for name in saves:
        scratch[name + "_new"] = pltpu.VMEM((T, B), f32) if name == "scale" else pltpu.VMEM((G, T, B), bf16)
    if turning:
        scratch["flipped"] = pltpu.VMEM((2, piece_size, B, B), bf16)
    if forward and tick < M:
        scratch["extra"] = pltpu.VMEM((T, B), f32)
    scratch["sems"] = pltpu.SemaphoreType.DMA((5,))
    if packs:
        scratch["pack_sems"] = pltpu.SemaphoreType.DMA((plan.bundle,))

    def kernel(*refs):
        ref = dict(zip(names, refs))
        rest = refs[len(names) + len(pack) + len(alias_from):]
        older_sent = refs[len(names):len(names) + len(pack)]
        out = dict(zip(out_names, rest))
        own = dict(zip(scratch, rest[len(out_names):]))
        tab, sent, acc, source, sems = ref["info"], out["sent"], own["acc"], own["source"], own["sems"]
        step = tick - LAG * tab[plan.section]
        active = (step >= 0) & (step < 2 * M)
        parity = tab[plan.section] % 2
        entry = (parity if forward else 1 - parity) * (G * B)
        packing = [pltpu.make_async_copy(old.at[pl.ds(0, G)], out["bundle"].at[i], own["pack_sems"].at[i]) for i, old in enumerate(older_sent)]
        for copy in packing:
            copy.start()

        def arriving(turn, unit, b):
            if use_entering:
                value = ref["entering"][unit, :, pl.ds(pl.multiple_of(entry + b * B, B), B)].astype(f32)
            if use_prev:
                older = ref["prev"][b].astype(f32)
                value = jnp.where(turn == first_turn, value, older) if use_entering else older
            if early:
                value = value + ref["early"][early_at, b].astype(f32)
            if critical:
                value = value + ref["critical"][b].astype(f32)
            return value.astype(bf16)

        def send(b, value):
            sent[b] = value
            if packs:
                out["bundle"][plan.bundle - 1, b] = value

        def keep(turn, unit, copies):
            for place, name in zip(turns_here, slots_of):
                @pl.when(turn == place)
                def _():
                    pltpu.make_async_copy(source, out[name].at[unit], sems.at[0]).start()
            for copy in copies:
                copy.start()
            acc[...] = jnp.zeros_like(acc)

        def multiply(turn):
            live = tab[turn]
            gather_at, scatter_at = (plan.rows_at, plan.cols_at) if forward else (plan.cols_at, plan.rows_at)
            if forward:
                first = turn * plan.slots
                tile_loop(tab, gather_at + first, scatter_at + first, live, G, source, ref["weights"], first, acc)
            for place in turns_here * (not forward):
                @pl.when(turn == place)
                def _():
                    first = place * plan.slots
                    tile_loop(tab, gather_at + first, scatter_at + first, live, G, source, ref["weights%d" % place], 0, acc)

        @pl.when(active)
        def _():
            turn = jnp.where(step >= M, 1, 0)
            unit = step - turn * M

            def gain(b):
                return ref["gains"][turn * G + b]

            if forward:
                kept, slope, scale = own["kept_new"], own["slope_new"], own["scale_new"]

                def enter(b, squares):
                    value = arriving(turn, unit, b)
                    kept[b] = value
                    value = value.astype(f32)
                    return squares + value * value

                square = lane_sum(each_block(G, enter, jnp.zeros((T, B), f32)))
                total = square
                if critical:
                    total = total + lane_sum(ref["critical"][G])
                if tick < M:
                    extra = own["extra"]
                    extra[...] = jnp.zeros_like(extra)

                    @pl.when(tab[plan.section] == 0)
                    def _():
                        def other(b, squares):
                            value = ref["entering"][unit, :, pl.ds(pl.multiple_of((G + b) * B, B), B)].astype(f32)
                            return squares + value * value

                        extra[...] = each_block(G, other, jnp.zeros((T, B), f32))

                    total = total + lane_sum(extra[...])
                inv_rms = lax.rsqrt(total / width + norm_eps)
                scale[...] = jnp.broadcast_to(inv_rms, (T, B))

                def normalize(b, carry):
                    source[b] = (kept[b].astype(f32) * inv_rms * gain(b)).astype(bf16)
                    return carry

                each_block(G, normalize)
                copies = [pltpu.make_async_copy(kept, out["kept_out"], sems.at[1]),
                          pltpu.make_async_copy(scale, out["scale_out"], sems.at[2])]
                keep(turn, unit, copies)
                multiply(turn)

                def activate(b, carry):
                    mixed = acc[b]
                    gate = jax.nn.sigmoid(mixed)
                    send(b, (mixed * gate).astype(bf16))
                    slope[b] = (gate * (1.0 + mixed * (1.0 - gate))).astype(bf16)
                    return carry

                half = G // 2
                for part in range(2):
                    each_block(half, lambda b, carry: activate(part * half + b, carry))
                    where = pl.ds(part * half, half)
                    copies.append(pltpu.make_async_copy(slope.at[where], out["slope_out"].at[where], sems.at[3 + part]))
                    copies[-1].start()
                sent[G] = split_pair(square, B)
            else:
                grad = own["grad_new"]

                def enter(b, carry):
                    value = arriving(turn, unit, b)
                    grad[b] = value
                    source[b] = (value.astype(f32) * ref["slope"][b].astype(f32)).astype(bf16)
                    return carry

                each_block(G, enter)
                copies = [pltpu.make_async_copy(grad, out["grad_out"], sems.at[1])]
                keep(turn, unit, copies)
                multiply(turn)

                def weigh(b, inner):
                    weighted = acc[b] * gain(b)
                    acc[b] = weighted
                    return inner + weighted * ref["kept"][b].astype(f32)

                inner = lane_sum(each_block(G, weigh, jnp.zeros((T, B), f32)))
                inv_rms = ref["scale"][:, 0:1]
                factor = inv_rms * inv_rms * inv_rms / width * inner
                total = factor
                if critical:
                    total = total + lane_sum(ref["critical"][G])

                def leave(b, carry):
                    send(b, (inv_rms * acc[b] - total * ref["kept"][b].astype(f32)).astype(bf16))
                    return carry

                each_block(G, leave)
                sent[G] = split_pair(factor, B)
            pltpu.make_async_copy(source, out[slots_of[0]].at[unit], sems.at[0]).wait()
            for copy in copies:
                copy.wait()

        @pl.when(jnp.logical_not(active))
        def _():
            sent[...] = jnp.zeros_like(sent)
            if packs:
                out["bundle"][plan.bundle - 1] = jnp.zeros((G, T, B), bf16)
            if turning:
                flipped = own["flipped"]

                rounds = piece_size // FLIP

                def flip(i, carry):
                    place = i // rounds
                    for k in range(FLIP):
                        at = (i - place * rounds) * FLIP + k
                        flipped[place, at] = ref["weights"][place * plan.slots + piece * share + at].T
                    return carry

                lax.fori_loop(0, 2 * rounds, flip, 0)
                moves = [pltpu.make_async_copy(
                    flipped.at[place], out["turned%d" % place].at[pl.ds(piece * share, piece_size)], sems.at[place])
                    for place in range(2)]
                for copy in moves:
                    copy.start()
                for copy in moves:
                    copy.wait()

        for copy in packing:
            copy.wait()

    ins = list(named.values()) + list(pack) + list(alias_from.values())
    outs = pl.pallas_call(
        kernel,
        in_specs=[SM] + [VM] * (len(names) - 1 + len(pack)) + [HBM] * len(alias_from),
        out_specs=[spec for spec, _ in shapes.values()],
        out_shape=[shape for _, shape in shapes.values()],
        input_output_aliases={len(names) + len(pack) + i: out_names.index(name) for i, name in enumerate(alias_from)},
        scratch_shapes=list(scratch.values()),
        compiler_params=pltpu.CompilerParams(vmem_limit_bytes=LIMIT),
        name="forward_tick" if forward else "backward_tick",
    )(*ins)
    return dict(zip(out_names, outs))


def tile_grads(plan, turn, info, normed_parts, error_parts, share, parts):
    G, T, B, M = plan.grid, plan.rows, plan.tile, plan.units
    local = plan.slots // parts
    steps = 4
    chunk = local // steps
    tokens = M * T

    def kernel(tab, *refs):
        normeds, errors = refs[:parts], refs[parts:2 * parts]
        out, turned, flat = refs[-3:]
        step = pl.program_id(0)

        @pl.when(step == 0)
        def _():
            def arrange(b, carry):
                for p in range(parts):
                    for m in range(M):
                        at = p * tokens + m * T
                        flat[b, at:at + T, :] = errors[p][m, b]
                    whole = jnp.concatenate([normeds[p][m, b] for m in range(M)], axis=0)
                    turned[b, :, p * tokens:(p + 1) * tokens] = whole.T
                return carry

            each_block(G, arrange)

        half = tab[plan.half]
        live = tab[turn]
        for k in range(chunk):
            i = step * chunk + k
            n = (i // share) * (share * parts) + half * share + i % share
            at = turn * plan.slots + n
            made = jnp.dot(turned[tab[plan.rows_at + at]], flat[tab[plan.cols_at + at]], preferred_element_type=f32)
            out[k] = jnp.where(n < live, made, 0.0).astype(bf16)

    whole = pl.BlockSpec((M, G, T, B), lambda i, *_: (0, 0, 0, 0))
    return pl.pallas_call(
        kernel,
        grid_spec=pltpu.PrefetchScalarGridSpec(
            num_scalar_prefetch=1,
            grid=(steps,),
            in_specs=[whole] * (2 * parts),
            out_specs=pl.BlockSpec((chunk, B, B), lambda i, *_: (i, 0, 0)),
            scratch_shapes=[pltpu.VMEM((G, B, parts * tokens), bf16), pltpu.VMEM((G, parts * tokens, B), bf16)],
        ),
        out_shape=pltpu.HBM((local, B, B), bf16),
        compiler_params=pltpu.CompilerParams(vmem_limit_bytes=GRAD_LIMIT),
        cost_estimate=pl.CostEstimate(flops=2 * local * B * B * parts * tokens, transcendentals=0, bytes_accessed=24 * 2**20),
        name="tile_grads",
    )(info, *normed_parts, *error_parts)


def sum_parts(parts):
    def kernel(given, out):
        total = given[0].astype(f32)
        for i in range(1, parts.shape[0]):
            total = total + given[i].astype(f32)
        out[...] = total.astype(bf16)

    rest = parts.shape[2:]
    return pl.pallas_call(
        kernel,
        grid=(parts.shape[1],),
        in_specs=[pl.BlockSpec((parts.shape[0], 1, *rest), lambda i: (0, i, 0, 0))],
        out_specs=pl.BlockSpec((1, *rest), lambda i: (i, 0, 0)),
        out_shape=jax.ShapeDtypeStruct(parts.shape[1:], bf16),
        compiler_params=pltpu.CompilerParams(vmem_limit_bytes=GRAD_LIMIT),
        name="sum_parts",
    )(parts)


def body(hidden_in, out_grad, gains, blocks, block_rows, block_cols, block_counts):
    sections = lax.axis_size("section")
    replicas = lax.axis_size("dp")
    section_pos = lax.axis_index("section").astype(jnp.int32)
    core = (lax.axis_index("dp") % PARTS).astype(jnp.int32)
    turns, slots, tile = blocks.shape[0], blocks.shape[2], blocks.shape[3]
    tokens = hidden_in.shape[0] * hidden_in.shape[1]
    half_width = hidden_in.shape[2] // 2
    grid = half_width // tile
    plan = Plan(sections, turns, slots, tile, grid, tokens)
    M, T = plan.units, plan.rows

    info = jnp.concatenate(
        [block_counts.reshape(-1), section_pos[None], core[None], block_rows.reshape(-1), block_cols.reshape(-1)]
    )
    entering = hidden_in.reshape(M, T, 2 * half_width)
    entering_grad = out_grad.reshape(M, T, 2 * half_width)
    weights = blocks.reshape(turns * slots, tile, tile)
    gain_rows = gains.reshape(turns * grid, 1, tile)

    def ring(part, by):
        return lax.ppermute(part, "section", [(i, (i + by) % sections) for i in range(sections)])

    def run(forward, weights, saved, hook):
        stores, turned = {}, [None, None]
        sents, ahead, bundles, kept = [], [], {}, []
        toward = 1 if forward else -1
        for order in range(plan.ticks):
            tick = order if forward else plan.ticks - 1 - order
            use_entering, use_prev = order < M + plan.span, order >= M
            named = dict(info=info, gains=gain_rows)
            if forward:
                named["weights"] = weights
            else:
                named["weights1"] = weights[1] if use_entering else None
                named["weights0"] = weights[0] if use_prev else None
            named["entering"] = (entering if forward else entering_grad) if use_entering else None
            if forward:
                named["prev"] = kept[order - M]["kept_out"] if use_prev else None
            else:
                named["kept"], named["slope"], named["scale"] = [saved[tick][name + "_out"] for name in ("kept", "slope", "scale")]
                named["prev"] = kept[order - M]["grad_out"] if use_prev else None
            named["critical"] = ahead[order - LAG] if order >= LAG else None
            named["early"] = bundles[-(-(order - plan.span) // plan.bundle)] if order >= plan.span else None
            pack = None
            if order % plan.bundle == 0 and order - plan.bundle + 1 + plan.span < plan.ticks:
                pack = tuple(sents[max(order - plan.bundle + 1, 0):order])
            made = tick_call(plan, tick, order, forward, named, stores, pack, turned, order == plan.ticks - 1)
            sents.append(made["sent"])
            kept.append(made)
            stores = stores | {name: made[name] for name in ("store0", "store1") if name in made}
            turned = [made.get("turned%d" % turn, turned[turn]) for turn in range(2)]
            ahead.append(ring(made["sent"], toward) if order + LAG < plan.ticks else None)
            if pack is not None:
                bundles[order // plan.bundle] = ring(made["bundle"], -toward)
            hook(order, ahead, stores)
        return kept, stores, turned

    saved, normed, turned = run(True, weights, None, lambda order, ahead, stores: None)

    members = replicas // PARTS
    share = slots // replicas
    alike = [[i for i in range(replicas) if i % PARTS == q] for q in range(PARTS)]

    def gather(own):
        return [own, lax.ppermute(own, "dp", [(i, i ^ 1) for i in range(replicas)])]

    def make_grads(turn, stores):
        name = "store%d" % turn
        return tile_grads(plan, turn, info, gather(normed[name]), gather(stores[name]), share, PARTS)

    def trade(part):
        return lax.all_to_all(
            part.reshape(members, share, tile, tile), "dp", 0, 0, axis_index_groups=alike, tiled=True
        )

    later = []

    def halfway(order, ahead, stores):
        if order == M + plan.span - 1:
            part, ahead[order] = lax.optimization_barrier((make_grads(1, stores), ahead[order]))
            later.append(lax.psum_scatter(part, "dp", scatter_dimension=0, axis_index_groups=alike, tiled=True))

    _, errors, _ = run(False, turned, saved, halfway)
    sooner = trade(make_grads(0, errors))
    return jnp.stack([sum_parts(sooner), later[0]])[:, None]


def solution(mesh):
    return jax.shard_map(
        body,
        mesh=mesh,
        in_specs=(
            P(None, "dp", None),
            P(None, "dp", None),
            P(None, "section", None),
            P(None, "section", None, None, None),
            P(None, "section", None),
            P(None, "section", None),
            P(None, "section"),
        ),
        out_specs=P(None, "section", "dp", None, None),
        check_vma=False,
    )
```
